256 devices in a mesh: row: 16 (over y, z_lo), col: 8 (over x, core), tp: 2 (over z_hi).
Axes of the slice: x: 4, y: 4, z: 8 (z_hi: 2, z_lo: 4; z = z_hi * 4 + z_lo), core: 2. Of those that a mesh axis runs over, the one named last changes fastest.
Arguments:
- gram: float32 [8, 16, 128, 1, 8, 2048], P(None, 'row', 'tp', None, 'col'), may hold values from -24 to 24
- inv_factor: bfloat16 [1024, 1024], replicated, as said below
- cross_gram: bfloat16 [8, 16, 128, 1024], P(None, 'row', 'tp'), may hold values from -24 to 24
- down_rows: bfloat16 [29568, 4096], P(('row', 'tp'), 'col'), may hold values from -0.03125 to 0.03125
- removed: int32 [1024], replicated, may hold values from 0 to 29567, as said below
Outputs:
- updated: float32 [8, 16, 128, 1, 8, 2048], P(None, 'row', 'tp', None, 'col')
- rhs_next: float32 [8, 16, 128, 4096], P(None, 'row', 'tp', 'col')
The draws below stay inside these ranges and needn't reach their ends.
Inputs may be any that keep to these rules, and one draw needn't show every extreme that they name: `inv_factor`: zero above the diagonal. `removed`: distinct ids in ascending order; among the neurons s * 924 to (s + 1) * 924 - 1 of any shard s at most 128 are listed, and one shard holds exactly 128.
All inputs are finite; a program needn't handle non-finite values.
Results may differ from the reference program's by a relative error of at most 0.0003.
Values may be sent and summed in bfloat16 or wider, within the bound.
A program may use at most 128 MiB of HBM per device.

```python
import jax
import jax.numpy as jnp
from jax import lax

FF = 29568
NR = 1024
DW = 4096
NB = 128
P_SIZE = 1024
CB = 2048
RC = 8
CCYC = 1
SHARDS = 32
FS = 924
CAP = 128
N_ROW = 16
N_COL = 8


def draw_inv_factor(key, part):
    values = jax.random.normal(key, (P_SIZE, P_SIZE), jnp.float32) * (0.176 / P_SIZE ** 0.5)
    lines = lax.broadcasted_iota(jnp.int32, (P_SIZE, P_SIZE), 0)
    places = lax.broadcasted_iota(jnp.int32, (P_SIZE, P_SIZE), 1)
    return jnp.where(places <= lines, values, 0.0).astype(jnp.bfloat16)


def draw_removed(key, part):
    key_hot, key_spots, key_pick = jax.random.split(key, 3)
    hottest = jax.random.randint(key_hot, (), 0, SHARDS)
    shard_keys = jax.random.split(key_spots, SHARDS)

    def spots_of(one_key):
        return jax.random.permutation(one_key, FS)[:CAP]
    spots = jax.vmap(spots_of)(shard_keys)
    order = (hottest + jnp.arange(SHARDS, dtype=jnp.int32)) % SHARDS
    neuron_ids = spots[order] + (order * FS)[:, None]
    others = neuron_ids[1:].reshape(-1)
    picked = jax.random.permutation(key_pick, (SHARDS - 1) * CAP)[:NR - CAP]
    chosen = jnp.concatenate([neuron_ids[0], others[picked]])
    return jnp.sort(chosen).astype(jnp.int32)


def shard_levels(key, dims, cuts, smallest, largest):
    factor_of, own = 1.0, jax.random.fold_in(key, 6)
    for dim, blocks in cuts:
        heights = jnp.exp(jax.random.uniform(jax.random.fold_in(own, dim), (blocks,), jnp.float32, smallest / len(cuts), largest / len(cuts)))
        factor_of = factor_of * jnp.repeat(heights, dims[dim] // blocks).reshape([-1 if axis == dim else 1 for axis in range(len(dims))])
    return factor_of


def centred(rng, shape, scale, limit, shards=(), held_as=jnp.bfloat16):
    entries = jax.random.normal(rng, shape, jnp.float32) * scale
    if len(shards) > 0:
        entries = shard_levels(rng, shape, shards, -0.22, 0.18) * entries
    return jnp.clip(entries, min=-limit, max=limit).astype(held_as)


def setup_inputs(seed: int = 0) -> dict:
    key_of = jax.random.split(jax.random.key(seed), 6)
    return {
        "gram": centred(key_of[0], (RC, N_ROW, NB, CCYC, N_COL, CB), 4.0, 24.0, ((1, 16), (2, 2), (4, 8)), jnp.float32),
        "inv_factor": draw_inv_factor(jax.random.fold_in(key_of[5], 71), 0),
        "cross_gram": centred(key_of[2], (RC, N_ROW, NB, NR), 4.0, 24.0, ((1, 16), (2, 2))),
        "down_rows": centred(key_of[3], (FF, DW), FF ** -0.5, 0.03125, ((0, 32), (1, 8))),
        "removed": draw_removed(jax.random.fold_in(key_of[5], 71), 0),
    }


def reference(gram, inv_factor, cross_gram, down_rows, removed):
    total = gram.shape[0] * gram.shape[1] * gram.shape[2]
    matrix = gram.reshape(total, total)
    factor = inv_factor.astype(jnp.float32)
    panel_factor = jnp.dot(matrix[:, :P_SIZE], factor.T, precision=lax.Precision.HIGHEST, preferred_element_type=jnp.float32)
    blocks = total // 1024 if total % 1024 == 0 else 1
    rows_each = total // blocks

    def update_block(index):
        start = (index * rows_each).astype(jnp.int32)
        stored = lax.dynamic_slice_in_dim(matrix, start, rows_each, 0)
        left = lax.dynamic_slice_in_dim(panel_factor, start, rows_each, 0)
        return stored - jnp.dot(left, panel_factor.T, precision=lax.Precision.HIGHEST, preferred_element_type=jnp.float32)

    updated = lax.map(update_block, jnp.arange(blocks, dtype=jnp.int32)).reshape(gram.shape)
    lost_rows = jnp.take(down_rows, removed.astype(jnp.int32), axis=0)
    cross = cross_gram.reshape(total, cross_gram.shape[3])
    rhs = jnp.dot(cross, lost_rows, preferred_element_type=jnp.float32)
    head = jnp.dot(factor, rhs[:P_SIZE], precision=lax.Precision.HIGHEST, preferred_element_type=jnp.float32)
    rhs_next = rhs - jnp.dot(panel_factor, head, precision=lax.Precision.HIGHEST, preferred_element_type=jnp.float32)
    return updated, rhs_next.reshape(cross_gram.shape[0], cross_gram.shape[1], cross_gram.shape[2], down_rows.shape[1])
```

```python
import jax
import jax.numpy as jnp
from jax import lax
from jax.experimental import pallas as pl
from jax.experimental.pallas import tpu as pltpu
from jax.sharding import PartitionSpec as P

NY, NZ, ZL = 4, 8, 4
BIAS = 32767.0


def plan(simple):
    found = []
    z_hops = [("z+", -1, 2), ("z-", 1, 2), ("z+", -2, 2), ("z-", 2, 2), ("z+", -3, 2), ("z-", 3, 2), ("z+", 4, 0), ("z-", 4, 1)]
    y_hops = [("y+", -1, 2), ("y-", 1, 2), ("y+", 2, 0), ("y-", 2, 1)]
    for way, a, half in y_hops:
        found.append((0, a, 0, way, half))
    for a in (0, -1, 1, 2):
        for way, b, half in z_hops:
            found.append((0, a, b, way, half))
    if not simple:
        for way, b, half in z_hops:
            found.append((1, 0, b, way, half))
        for b in (0, -1, 1, -2, 2, -3, 3, 4):
            for way, a, half in y_hops:
                found.append((1, a, b, way, half))
    else:
        found = [t for t in found if t[4] != 1]
    return found


def sender_chunk(t):
    part, a, b, way, half = t
    if way == "y+":
        return (part, {-1: 0, 2: -1}[a], b)
    if way == "y-":
        return (part, {1: 0, 2: 1}[a], b)
    if way == "z+":
        return (part, a, {-1: 0, -2: -1, -3: -2, 4: -3}[b])
    return (part, a, {1: 0, 2: 1, 3: 2, 4: 3}[b])


class Stream:
    def __init__(self, buf, send, recv, rows, simple):
        self.buf, self.send, self.recv, self.rows, self.simple = buf, send, recv, rows, simple
        self.moves = plan(simple)

    def piece(self, t, slot):
        part, half = t[0], t[4]
        if self.simple:
            return self.buf.at[slot]
        start, count = self.rows[part][half]
        return self.buf.at[slot, pl.ds(start, count)]


def comm_kernel(lsrc, ssrc, lost, c0own, lall, sall, ball, c0all, lrow, srow, c0full,
                l_send, l_recv, s_send, s_recv, b_send, b_recv, c_send, c_recv, x_send, x_recv):
    row, col, tp = lax.axis_index("row"), lax.axis_index("col"), lax.axis_index("tp")
    y, z = row // ZL, tp * ZL + row % ZL

    def slot_of(a, b):
        yy, zz = lax.rem(y + a + NY, NY), lax.rem(z + b + NZ, NZ)
        return yy * 8 + lax.rem(zz, ZL) * 2 + zz // ZL

    def device_of(a, b):
        yy, zz = lax.rem(y + a + NY, NY), lax.rem(z + b + NZ, NZ)
        return {"row": yy * ZL + lax.rem(zz, ZL), "col": col, "tp": zz // ZL}

    to = {"y+": device_of(1, 0), "y-": device_of(-1, 0), "z+": device_of(0, 1), "z-": device_of(0, -1)}
    mine = slot_of(0, 0)

    def at_col(c):
        return {"row": row, "col": c, "tp": tp}

    barrier = pltpu.get_barrier_semaphore()
    for dev in to.values():
        pl.semaphore_signal(barrier, inc=1, device_id=dev, device_id_type=pl.DeviceIdType.MESH)
    for off in range(1, 8):
        pl.semaphore_signal(barrier, inc=1, device_id=at_col(lax.rem(col + off, 8)), device_id_type=pl.DeviceIdType.MESH)
    pl.semaphore_wait(barrier, 11)

    c_st = Stream(c0all, c_send, c_recv, None, True)
    b_st = Stream(ball, b_send, b_recv, {0: {0: (0, 32), 1: (32, 32), 2: (0, 64)}, 1: {0: (64, 32), 1: (96, 32), 2: (64, 64)}}, False)
    l_st = Stream(lall, l_send, l_recv, {0: {0: (0, 32), 1: (32, 16), 2: (0, 48)}, 1: {0: (48, 32), 1: (80, 48), 2: (48, 80)}}, False)
    s_st = Stream(sall, s_send, s_recv, None, True)
    started = []

    def copy_of(st, i, slot):
        t = st.moves[i]
        return pltpu.make_async_remote_copy(
            src_ref=st.piece(t, slot), dst_ref=st.piece(t, slot), send_sem=st.send.at[i], recv_sem=st.recv.at[i],
            device_id=to[t[3]], device_id_type=pl.DeviceIdType.MESH)

    def start_from(st, chunk):
        for i, t in enumerate(st.moves):
            if sender_chunk(t) == chunk:
                c = copy_of(st, i, slot_of(chunk[1], chunk[2]))
                c.start()
                started.append(c)

    def wait_for(st, chunk):
        for i, t in enumerate(st.moves):
            if t[:3] == chunk:
                copy_of(st, i, slot_of(chunk[1], chunk[2])).wait_recv()

    def hand_out(c, wait):
        for k, (src, dst, n) in enumerate(((lsrc, lall, 0), (ssrc, sall, 7))):
            cp = pltpu.make_async_remote_copy(
                src_ref=src.at[c], dst_ref=dst.at[mine], send_sem=x_send.at[n + c - 1], recv_sem=x_recv.at[k],
                device_id=at_col(c), device_id_type=pl.DeviceIdType.MESH)
            if wait:
                cp.wait_send()
            else:
                cp.start()

    @pl.when(col == 0)
    def _():
        for c in (4, 2, 6, 5, 3, 7, 1):
            hand_out(c, False)

    c0all[mine] = c0own[...]
    ball[mine] = lost[...]
    start_from(c_st, (0, 0, 0))
    start_from(b_st, (0, 0, 0))
    start_from(b_st, (1, 0, 0))

    def peer_copies(n, src, dst_of):
        copies = []
        for off in range(1, 8):
            cp = pltpu.make_async_remote_copy(
                src_ref=src, dst_ref=dst_of.at[col], send_sem=x_send.at[14 + 7 * n + off - 1], recv_sem=x_recv.at[2 + 7 * n + off - 1],
                device_id=at_col(lax.rem(col + off, 8)), device_id_type=pl.DeviceIdType.MESH)
            cp.start()
            copies.append(cp)
        return copies

    def own_rows():
        @pl.when(col == 0)
        def _():
            lall[mine] = lsrc[0]
            sall[mine] = ssrc[0]

        @pl.when(col != 0)
        def _():
            for k, dst in enumerate((lall, sall)):
                pltpu.make_async_remote_copy(
                    src_ref=dst.at[mine], dst_ref=dst.at[mine], send_sem=x_send.at[0], recv_sem=x_recv.at[k],
                    device_id=to["y+"], device_id_type=pl.DeviceIdType.MESH).wait_recv()

    peers = []
    events = []
    for st, offset in ((c_st, 0), (b_st, 0), (l_st, 1.5), (s_st, 1.5)):
        for chunk in sorted({t[:3] for t in st.moves}):
            events.append((abs(chunk[1]) + abs(chunk[2]) + offset, st, chunk))
    events.sort(key=lambda e: e[0])
    begun, c0_left = False, 31
    for when, st, chunk in events:
        if when > 1 and not begun:
            begun = True
            own_rows()
            lrow[col] = lall[mine]
            srow[col] = sall[mine]
            for part in (0, 1):
                start_from(l_st, (part, 0, 0))
            start_from(s_st, (0, 0, 0))
            peers += peer_copies(0, lall.at[mine], lrow)
            peers += peer_copies(1, sall.at[mine], srow)
        wait_for(st, chunk)
        start_from(st, chunk)
        if st is c_st:
            c0_left -= 1
            if c0_left == 0:
                c0full[col] = c0all[0:16]
                peers += peer_copies(2, c0full.at[col], c0full)
    for c in started:
        c.wait_send()
    for c in peers:
        c.wait_send()
        c.wait_recv()

    @pl.when(col == 0)
    def _():
        for c in range(1, 8):
            hand_out(c, True)


def communicate(lsrc, ssrc, lost, c0own):
    n = lambda simple: len(plan(simple))
    f, bf, i16 = jnp.float32, jnp.bfloat16, jnp.int16
    vm = pl.BlockSpec(memory_space=pltpu.VMEM)
    dma = pltpu.SemaphoreType.DMA
    return pl.pallas_call(
        comm_kernel,
        out_shape=[
            jax.ShapeDtypeStruct((32, 128, 512), i16),
            jax.ShapeDtypeStruct((32, 8, 128), f),
            jax.ShapeDtypeStruct((32, 128, 512), bf),
            jax.ShapeDtypeStruct((32, 16, 512), bf),
            jax.ShapeDtypeStruct((8, 128, 512), i16),
            jax.ShapeDtypeStruct((8, 8, 128), f),
            jax.ShapeDtypeStruct((8, 16, 16, 512), bf),
        ],
        in_specs=[vm] * 4,
        out_specs=[vm] * 7,
        scratch_shapes=[dma((n(False),)), dma((n(False),)), dma((n(True),)), dma((n(True),)),
                        dma((n(False),)), dma((n(False),)), dma((n(True),)), dma((n(True),)),
                        dma((35,)), dma((23,))],
        compiler_params=pltpu.CompilerParams(collective_id=0, has_side_effects=True, vmem_limit_bytes=48 << 20),
    )(lsrc, ssrc, lost, c0own)


def split2(v):
    hi = lax.reduce_precision(v, 8, 7)
    return hi.astype(jnp.bfloat16), (v - hi).astype(jnp.bfloat16)


def dot(a, b, dims):
    return lax.dot_general(a, b, (dims, ((), ())), preferred_element_type=jnp.float32)


def dot3(a, b, dims):
    (ah, al), (bh, bl) = split2(a), split2(b)
    return dot(ah, bh, dims) + (dot(ah, bl, dims) + dot(al, bh, dims))


def per_device(gram, inv_factor, cross_gram, down_rows, removed):
    f, bf = jnp.float32, jnp.bfloat16
    nt, nn = ((1,), (1,)), ((1,), (0,))
    grid = gram.reshape(512, 2048)
    ph, pl_ = split2(grid[:, :1024])
    left = dot(ph, inv_factor, nt) + dot(pl_, inv_factor, nt)
    scale = jnp.maximum(jnp.max(jnp.abs(left), axis=1), 1e-30) / BIAS
    q = jnp.round(left / scale[:, None]).astype(jnp.int16)
    lsrc = q.reshape(8, 64, 2, 512).transpose(0, 2, 1, 3).reshape(8, 128, 512)
    ssrc = jnp.broadcast_to(jnp.pad(scale.reshape(8, 1, 64), ((0, 0), (0, 0), (0, 64))), (8, 8, 128))
    col = lax.axis_index("col")
    member = lax.axis_index(("row", "tp"))
    owner = removed // 924
    own_start = jnp.sum(owner < member)
    slot = jnp.arange(1024) - own_start
    local = removed - member * 924
    slot = jnp.where(owner == member, slot, -1)
    pick = (jnp.arange(128)[:, None] == slot[None, :]).astype(bf)
    place = (local[:, None] == jnp.arange(924)[None, :]).astype(bf)
    onehot = dot(pick, place, nn).astype(bf)
    lost = dot(onehot, down_rows, nn).astype(bf)
    c0own = lax.dynamic_slice_in_dim(cross_gram[0, 0], col * 8, 8, 0)
    c0own = c0own.reshape(8, 2, 512).transpose(1, 0, 2).reshape(16, 512)
    lall, sall, ball, _, lrow, srow, c0full = communicate(lsrc, ssrc, lost, c0own)

    def whole(qq, ss):
        n = qq.shape[0]
        v = qq.reshape(n, 2, 64, 512).transpose(0, 2, 1, 3).reshape(n * 64, 1024).astype(f)
        return v * ss[:, 0, :64].reshape(n * 64, 1)

    rows, cols = whole(lrow, srow), whole(lall, sall)
    updated = grid - dot3(rows, cols, nt)
    earlier = jnp.sum(owner[None, :] < owner[:, None], axis=1)
    where = owner * 128 + jnp.arange(1024) - earlier
    lost_rows = dot((where[:, None] == jnp.arange(4096)[None, :]).astype(bf), ball.reshape(4096, 512), nn).astype(bf)
    c0 = c0full.reshape(8, 16, 2, 8, 512).transpose(1, 0, 3, 2, 4).reshape(1024, 1024)
    cross = cross_gram.reshape(512, 1024)
    rhs = dot(cross, lost_rows, nn)
    rhs0 = dot(c0, lost_rows, nn)
    rh, rl = split2(rhs0)
    head = dot(inv_factor, rh, nn) + dot(inv_factor, rl, nn)
    rhs_next = rhs - dot3(rows, head, nn)
    return (updated.reshape(gram.shape), rhs_next.reshape(8, 1, 64, 512))


def solution(mesh):
    return jax.shard_map(
        per_device,
        mesh=mesh,
        in_specs=(
            P(None, "row", "tp", None, "col", None),
            P(),
            P(None, "row", "tp", None),
            P(("row", "tp"), "col"),
            P(),
        ),
        out_specs=(P(None, "row", "tp", None, "col", None), P(None, "row", "tp", "col")),
        check_vma=False,
    )
```

```python
import jax
import jax.numpy as jnp
from jax import lax
from jax.experimental import pallas as pl
from jax.experimental.pallas import tpu as pltpu
from jax.sharding import PartitionSpec as P

NY, NZ, ZL = 4, 8, 4
MESH = pl.DeviceIdType.MESH
F32, BF16, I16 = jnp.float32, jnp.bfloat16, jnp.int16
NT, NN, TN = ((1,), (1,)), ((1,), (0,)), ((0,), (0,))
Z_HOPS = [("z+", -1, 2), ("z-", 1, 2), ("z+", -2, 2), ("z-", 2, 2), ("z+", -3, 2), ("z-", 3, 2), ("z+", 4, 0), ("z-", 4, 1)]
Y_HOPS = [("y+", -1, 2), ("y-", 1, 2), ("y+", 2, 0), ("y-", 2, 1)]


def plan(simple):
    found = [(0, a, 0, way, half) for way, a, half in Y_HOPS]
    found += [(0, a, b, way, half) for a in (0, -1, 1, 2) for way, b, half in Z_HOPS]
    if simple:
        return [t for t in found if t[4] != 1]
    found += [(1, 0, b, way, half) for way, b, half in Z_HOPS]
    return found + [(1, a, b, way, half) for b in (0, -1, 1, -2, 2, -3, 3, 4) for way, a, half in Y_HOPS]


def plan_y():
    return [(0, a, 0, way, half) for way, a, half in Y_HOPS]


def sender_chunk(t):
    part, a, b, way, half = t
    if way == "y+":
        return (part, {-1: 0, 2: -1}[a], b)
    if way == "y-":
        return (part, {1: 0, 2: 1}[a], b)
    if way == "z+":
        return (part, a, {-1: 0, -2: -1, -3: -2, 4: -3}[b])
    return (part, a, {1: 0, 2: 1, 3: 2, 4: 3}[b])


L_ROWS = {0: {0: (0, 32), 1: (32, 16), 2: (0, 48)}, 1: {0: (48, 32), 1: (80, 48), 2: (48, 80)}}
Y_ROWS = {0: {0: (0, 128), 1: (128, 128), 2: (0, 256)}}


def dot(a, b, dims):
    return lax.dot_general(a, b, (dims, ((), ())), preferred_element_type=F32)


def split2(v):
    hi = v.astype(BF16)
    return hi, (v - hi.astype(F32)).astype(BF16)


def iota(shape, axis):
    return lax.broadcasted_iota(jnp.int32, shape, axis)


def kernel(gram, inv, cross_h, down, removed, updated, rhs_out,
           gt, m_ref, cross, c0own, lsrc, ssrc, lall, sall, lrow, srow, rh, rl, ch, cl,
           c0all, c0full, pack, yslot, fbuf, zslot, lost, rhs0, hh, hl,
           g_sem, in_sem, o_sem, l_send, l_recv, s_send, s_recv, c_send, c_recv, x_send, x_recv,
           p_send, p_recv, y_send, y_recv):
    row, col, tp = lax.axis_index("row"), lax.axis_index("col"), lax.axis_index("tp")
    y, z = row // ZL, tp * ZL + lax.rem(row, ZL)
    xx, core = col // 2, lax.rem(col, 2)

    def slot_of(a, b):
        yy, zz = lax.rem(y + a + NY, NY), lax.rem(z + b + NZ, NZ)
        return yy * 8 + lax.rem(zz, ZL) * 2 + zz // ZL

    def device_of(a, b):
        yy, zz = lax.rem(y + a + NY, NY), lax.rem(z + b + NZ, NZ)
        return {"row": yy * ZL + lax.rem(zz, ZL), "col": col, "tp": zz // ZL}

    def at_col(c):
        return {"row": row, "col": c, "tp": tp}

    def peer_col(off):
        return lax.rem(xx + off, 4) * 2 + core

    to = {"y+": device_of(1, 0), "y-": device_of(-1, 0), "z+": device_of(0, 1), "z-": device_of(0, -1)}
    mine = slot_of(0, 0)

    def remote(src, dst, send, recv, dev):
        return pltpu.make_async_remote_copy(src_ref=src, dst_ref=dst, send_sem=send, recv_sem=recv, device_id=dev, device_id_type=MESH)

    loads = [pltpu.make_async_copy(gram.at[:, j, :], gt.at[j], g_sem.at[j]) for j in range(16)]
    c0load = pltpu.make_async_copy(
        cross_h.at[pl.ds(pl.multiple_of(16 * xx, 16), 16), pl.ds(pl.multiple_of(512 * core, 512), 512)], c0own, in_sem.at[0])
    m_load = pltpu.make_async_copy(inv, m_ref, in_sem.at[1])
    x_load = pltpu.make_async_copy(cross_h, cross, in_sem.at[2])
    c0load.start()
    for j in range(8):
        loads[j].start()
    m_load.start()
    for j in range(8, 16):
        loads[j].start()
    x_load.start()

    barrier = pltpu.get_barrier_semaphore()
    others = [device_of(a, 0) for a in (1, 2, 3)] + [device_of(0, b) for b in range(1, 8)]
    others += [at_col(lax.rem(col + off, 8)) for off in range(1, 8)]
    for dev in others:
        pl.semaphore_signal(barrier, inc=1, device_id=dev, device_id_type=MESH)
    pl.semaphore_wait(barrier, len(others))

    class Stream:
        def __init__(self, buf, send, recv, rows, moves):
            self.buf, self.send, self.recv, self.rows, self.moves = buf, send, recv, rows, moves

        def piece(self, t, slot):
            if self.rows is None:
                return self.buf.at[slot]
            start, count = self.rows[t[0]][t[4]]
            return self.buf.at[slot, pl.ds(start, count)]

        def slot(self, a, b):
            return slot_of(a, b)

    class YStream(Stream):
        def slot(self, a, b):
            return lax.rem(y + a + NY, NY)

    c_st = Stream(c0all, c_send, c_recv, None, plan(True))
    l_st = Stream(lall, l_send, l_recv, L_ROWS, plan(False))
    s_st = Stream(sall, s_send, s_recv, None, plan(True))
    y_st = YStream(lost, y_send, y_recv, Y_ROWS, plan_y())
    started = []

    def copy_of(st, i, slot):
        t = st.moves[i]
        return remote(st.piece(t, slot), st.piece(t, slot), st.send.at[i], st.recv.at[i], to[t[3]])

    def start_from(st, chunk):
        for i, t in enumerate(st.moves):
            if sender_chunk(t) == chunk:
                c = copy_of(st, i, st.slot(chunk[1], chunk[2]))
                c.start()
                started.append(c)

    def wait_for(st, chunk):
        for i, t in enumerate(st.moves):
            if t[:3] == chunk:
                copy_of(st, i, st.slot(chunk[1], chunk[2])).wait_recv()

    def many(copies):
        for c in copies:
            c.start()
        started.extend(copies)
        return copies

    c0load.wait()
    c0all[mine] = c0own[...]
    start_from(c_st, (0, 0, 0))

    def hand_out(c):
        return [remote(lsrc.at[c], lall.at[mine], x_send.at[c - 1], x_recv.at[0], at_col(c)),
                remote(ssrc.at[c], sall.at[mine], x_send.at[7 + c - 1], x_recv.at[1], at_col(c))]

    eye = iota((64, 128), 0) == iota((64, 128), 1)

    @pl.when(col == 0)
    def _():
        for j in range(8):
            loads[j].wait()
        m_load.wait()
        for first in (4, 0):
            r0 = first * 64
            parts = [split2(gt[j, r0:r0 + 256, :]) for j in range(8)]
            hi = jnp.concatenate([p[0] for p in parts], axis=1)
            lo = jnp.concatenate([p[1] for p in parts], axis=1)
            both = jnp.concatenate([hi, lo], axis=0)
            blocks = []
            for n in range(4):
                k = 256 * (n + 1)
                d = dot(both[:, :k], m_ref[256 * n:256 * n + 256, :k], NT)
                blocks.append(d[:256] + d[256:])
            top = jnp.maximum(blocks[0], -blocks[0])
            for b in blocks[1:]:
                top = jnp.maximum(top, jnp.abs(b))
            scale = jnp.maximum(jnp.max(top, axis=1, keepdims=True), 1e-30) / 32767.0
            inverse = 1.0 / scale
            for i in range(4):
                c = first + i
                rows = slice(64 * i, 64 * i + 64)
                for n in range(4):
                    q = lax.round(blocks[n][rows] * inverse[rows], lax.RoundingMethod.TO_NEAREST_EVEN)
                    q = jnp.clip(q, -32767.0, 32767.0).astype(jnp.int32).astype(I16)
                    half, lane = n // 2, 256 * (n % 2)
                    lsrc[c, 64 * half:64 * half + 64, lane:lane + 256] = q
                lanes = jnp.sum(jnp.where(eye, jnp.broadcast_to(scale[rows], (64, 128)), 0.0), axis=0, keepdims=True)
                ssrc[c] = jnp.broadcast_to(lanes, (8, 128))
            for c in ((4, 6, 5, 7) if first == 4 else (2, 3, 1)):
                for cp in hand_out(c):
                    cp.start()

    rem = removed[...]
    flat = jnp.concatenate([rem[i:i + 1, :] for i in range(8)], axis=1)

    def first_of(base):
        less = jnp.where(rem < base, 1.0, 0.0)
        return jnp.sum(jnp.sum(less, axis=1, keepdims=True), axis=0, keepdims=True).astype(jnp.int32)

    shard = down.shape[0]
    base = mine * shard
    place = jnp.where(iota((shard, 1024), 0) == flat - base, 1.0, 0.0).astype(BF16)
    order = jnp.where(iota((128, 1024), 1) - first_of(base) == iota((128, 1024), 0), 1.0, 0.0).astype(BF16)
    pick = dot(order, place, NT).astype(BF16)
    pack[...] = dot(pick, down[...], NN).astype(BF16)
    yslot[y] = pack[...]
    ph1 = many([remote(pack, yslot.at[y], p_send.at[a - 1], p_recv.at[a - 1], device_of(a, 0)) for a in (1, 2, 3)])

    def phase_f():
        for c in ph1:
            c.wait_recv()
        seg = jnp.concatenate([removed[pl.ds(2 * y + i, 1), :] for i in range(2)], axis=1)
        picks = []
        for yy in range(4):
            b = (yy * 8 + lax.rem(mine, 8)) * shard
            inside = (seg >= b) & (seg < b + shard)
            at = jnp.where(inside, iota((1, 256), 1) + 256 * y - first_of(b), -1)
            picks.append(jnp.where(iota((128, 256), 0) == at, 1.0, 0.0).astype(BF16))
        f = dot(jnp.concatenate(picks, axis=0), yslot[...].reshape(512, 512), TN).astype(BF16)
        for i in range(8):
            fbuf[i] = f[32 * i:32 * i + 32]
        zslot[z] = fbuf[z]
        return many([remote(fbuf.at[lax.rem(z + b, 8)], zslot.at[z], p_send.at[3 + b - 1], p_recv.at[3 + b - 1], device_of(0, b))
                     for b in range(1, 8)])

    def phase_r(ph2):
        for c in ph2:
            c.wait_recv()
        total = zslot[0].astype(F32)
        for i in range(1, 8):
            total = total + zslot[i].astype(F32)
        here = pl.ds(pl.multiple_of(32 * z, 32), 32)
        lost[y, here, :] = total.astype(BF16)
        return many([remote(lost.at[y, here], lost.at[y, here], p_send.at[10 + b - 1], p_recv.at[10 + b - 1], device_of(0, b))
                     for b in range(1, 8)])

    def x_peers(n, src, dst):
        return many([remote(src, dst.at[col], x_send.at[14 + 7 * n + off - 1], x_recv.at[2 + 7 * n + off - 1], at_col(peer_col(off)))
                     for off in range(1, 4)])

    def to_sibling(n, off, src, dst, slot):
        return many([remote(src, dst.at[slot], x_send.at[14 + 7 * n + 3 + off], x_recv.at[2 + 7 * n + 3 + off], at_col(col + 1 - 2 * core))])

    state = {}

    def own_rows():
        @pl.when(col == 0)
        def _():
            lall[mine] = lsrc[0]
            sall[mine] = ssrc[0]

        @pl.when(col != 0)
        def _():
            for k, dst in enumerate((lall, sall)):
                remote(dst.at[mine], dst.at[mine], x_send.at[0], x_recv.at[k], to["y+"]).wait_recv()
        for part in (0, 1):
            start_from(l_st, (part, 0, 0))
        start_from(s_st, (0, 0, 0))
        lrow[col] = lall[mine]
        srow[col] = sall[mine]
        state["xl"] = x_peers(0, lrow.at[col], lrow)
        state["xs"] = x_peers(1, srow.at[col], srow)
        state["sl"] = to_sibling(0, 0, lrow.at[col], lrow, col)
        state["ss"] = to_sibling(1, 0, srow.at[col], srow, col)

    def forward_rows(n, key, skey, buf):
        for off in range(1, 4):
            state[key][off - 1].wait_recv()
            c = lax.rem(xx - off + 4, 4) * 2 + core
            state[skey] += to_sibling(n, off, buf.at[c], buf, c)

    def dequant(q_ref, s_ref, slot):
        s = jnp.sum(jnp.where(eye, jnp.broadcast_to(s_ref[slot, 0:1, :], (64, 128)), 0.0), axis=1, keepdims=True)
        v = jnp.concatenate([q_ref[slot, 0:64, :], q_ref[slot, 64:128, :]], axis=1)
        return split2(v.astype(jnp.int32).astype(F32) * s)

    def rows_ready():
        for k in ("sl", "ss"):
            for c in state[k]:
                c.wait_recv()

        def body(c, _):
            hi, lo = dequant(lrow, srow, c)
            at = pl.ds(pl.multiple_of(64 * c, 64), 64)
            rh[at, :] = hi
            rl[at, :] = lo
            return 0
        lax.fori_loop(0, 8, body, 0)

    outs = []

    def columns(stage, a):
        yy = lax.rem(y + a + NY, NY)

        def body(g, _):
            for i in range(4):
                hi, lo = dequant(lall, sall, yy * 8 + 4 * g + i)
                ch[64 * i:64 * i + 64, :] = hi
                cl[64 * i:64 * i + 64, :] = lo
            p = dot(rh[...], ch[...], NT) + dot(rh[...], cl[...], NT) + dot(rl[...], ch[...], NT)
            for i in range(2):
                j = yy * 4 + 2 * g + i
                gt[j] = gt[j] - p[:, 128 * i:128 * i + 128]
                pltpu.make_async_copy(gt.at[j], updated.at[:, j, :], o_sem.at[stage * 4 + 2 * g + i]).start()
            return 0
        lax.fori_loop(0, 2, body, 0)

    def columns_sent():
        for stage, a in enumerate((0, -1, 1, 2)):
            yy = lax.rem(y + a + NY, NY)
            for i in range(4):
                j = yy * 4 + i
                pltpu.make_async_copy(gt.at[j], updated.at[:, j, :], o_sem.at[stage * 4 + i]).wait()

    def right_side():
        for c in state["sc"]:
            c.wait_recv()
        x_load.wait()
        for x4 in range(4):
            r = None
            for k in range(2):
                block = dot(c0full[2 * x4 + k].reshape(256, 512), lost[2 * k:2 * k + 2].reshape(512, 512), NN)
                r = block if r is None else r + block
            for m in range(16):
                rhs0[64 * m + 16 * x4:64 * m + 16 * x4 + 16, :] = r[16 * m:16 * m + 16]
        r_hi, r_lo = split2(rhs0[...])
        for n in range(4):
            k = 256 * (n + 1)
            mm = m_ref[256 * n:256 * n + 256, :k]
            hi, lo = split2(dot(mm, r_hi[:k], NN) + dot(mm, r_lo[:k], NN))
            hh[256 * n:256 * n + 256, :] = hi
            hl[256 * n:256 * n + 256, :] = lo
        rhs = dot(cross[...], lost[...].reshape(1024, 512), NN)
        rhs_out[...] = rhs - (dot(rh[...], hh[...], NN) + dot(rh[...], hl[...], NN) + dot(rl[...], hh[...], NN))

    def c0_done():
        c0full[col] = c0all[0:16]
        state["xc"] = x_peers(2, c0full.at[col], c0full)
        state["sc"] = to_sibling(2, 0, c0full.at[col], c0full, col)

    def loaded():
        @pl.when(col != 0)
        def _():
            for j in range(8):
                loads[j].wait()
            m_load.wait()
        for j in range(8, 16):
            loads[j].wait()

    def done_r():
        for c in state["ph3"]:
            c.wait_recv()
        start_from(y_st, (0, 0, 0))

    def y_one():
        for a in (-1, 1):
            wait_for(y_st, (0, a, 0))
            start_from(y_st, (0, a, 0))

    events = []
    for chunk in sorted({t[:3] for t in c_st.moves}):
        events.append((4 + 2 * (abs(chunk[1]) + abs(chunk[2])), 1, lambda chunk=chunk: (wait_for(c_st, chunk), start_from(c_st, chunk))))
    for st in (s_st, l_st):
        for chunk in sorted({t[:3] for t in st.moves}):
            events.append((10 + 5 * (abs(chunk[1]) + abs(chunk[2])), 2,
                           lambda st=st, chunk=chunk: (wait_for(st, chunk), start_from(st, chunk))))
    events.append((8.5, 0, lambda: state.update(ph2=phase_f())))
    events.append((10.5, 0, own_rows))
    events.append((14.5, 0, lambda: state.update(ph3=phase_r(state["ph2"]))))
    events.append((16.5, 0, c0_done))
    events.append((17, 0, lambda: forward_rows(1, "xs", "ss", srow)))
    events.append((19, 0, lambda: forward_rows(0, "xl", "sl", lrow)))
    events.append((19.5, 0, done_r))
    events.append((22, 0, loaded))
    events.append((22.5, 0, rows_ready))
    events.append((25.5, 0, y_one))
    events.append((26, 0, lambda: forward_rows(2, "xc", "sc", c0full)))
    events.append((31, 0, lambda: (wait_for(y_st, (0, 2, 0)), right_side())))
    events.append((32, 0, lambda: columns(0, 0)))
    events.append((37, 0, lambda: columns(1, -1)))
    events.append((38, 0, lambda: columns(2, 1)))
    events.append((45, 0, lambda: columns(3, 2)))
    events.sort(key=lambda e: (e[0], e[1]))
    for e in events:
        e[2]()
    for c in started:
        c.wait_send()
    columns_sent()

    @pl.when(col == 0)
    def _():
        for c in range(1, 8):
            for cp in hand_out(c):
                cp.wait_send()


def per_device(gram, inv_factor, cross_gram, down_rows, removed):
    vm = pl.BlockSpec(memory_space=pltpu.VMEM)
    hbm = pl.BlockSpec(memory_space=pl.ANY)
    dma = pltpu.SemaphoreType.DMA
    big, small = len(plan(False)), len(plan(True))
    v = pltpu.VMEM
    updated, rhs = pl.pallas_call(
        kernel,
        out_shape=[jax.ShapeDtypeStruct((512, 16, 128), F32), jax.ShapeDtypeStruct((512, 512), F32)],
        in_specs=[hbm, hbm, hbm, vm, vm],
        out_specs=[hbm, vm],
        scratch_shapes=[
            v((16, 512, 128), F32), v((1024, 1024), BF16), v((512, 1024), BF16), v((16, 512), BF16),
            v((8, 128, 512), I16), v((8, 8, 128), F32), v((32, 128, 512), I16), v((32, 8, 128), F32),
            v((8, 128, 512), I16), v((8, 8, 128), F32), v((512, 1024), BF16), v((512, 1024), BF16),
            v((256, 1024), BF16), v((256, 1024), BF16),
            v((32, 16, 512), BF16), v((8, 16, 16, 512), BF16), v((128, 512), BF16), v((4, 128, 512), BF16),
            v((8, 32, 512), BF16), v((8, 32, 512), BF16), v((4, 256, 512), BF16),
            v((1024, 512), F32), v((1024, 512), BF16), v((1024, 512), BF16),
            dma((16,)), dma((3,)), dma((16,)), dma((big,)), dma((big,)), dma((small,)), dma((small,)),
            dma((small,)), dma((small,)), dma((35,)), dma((23,)), dma((17,)), dma((17,)), dma((4,)), dma((4,)),
        ],
        compiler_params=pltpu.CompilerParams(collective_id=0, has_side_effects=True, vmem_limit_bytes=56 << 20),
    )(gram.reshape(512, 16, 128), inv_factor, cross_gram.reshape(512, 1024), down_rows, removed.reshape(8, 128))
    return (updated.reshape(gram.shape), rhs.reshape(8, 1, 64, 512))


def solution(mesh):
    return jax.shard_map(
        per_device,
        mesh=mesh,
        in_specs=(
            P(None, "row", "tp", None, "col", None),
            P(),
            P(None, "row", "tp", None),
            P(("row", "tp"), "col"),
            P(),
        ),
        out_specs=(P(None, "row", "tp", None, "col", None), P(None, "row", "tp", "col")),
        check_vma=False,
    )
```

```python
import jax
import jax.numpy as jnp
from jax import lax
from jax.experimental import pallas as pl
from jax.experimental.pallas import tpu as pltpu
from jax.sharding import PartitionSpec as P

NY, NZ, ZL = 4, 8, 4
MESH = pl.DeviceIdType.MESH
F32, BF16, I16 = jnp.float32, jnp.bfloat16, jnp.int16
NT, NN, TN = ((1,), (1,)), ((1,), (0,)), ((0,), (0,))
Z_HOPS = [("z+", -1, 2), ("z-", 1, 2), ("z+", -2, 2), ("z-", 2, 2), ("z+", -3, 2), ("z-", 3, 2), ("z+", 4, 0), ("z-", 4, 1)]
Y_HOPS = [("y+", -1, 2), ("y-", 1, 2), ("y+", 2, 0), ("y-", 2, 1)]


def plan(simple):
    found = [(0, a, 0, way, half) for way, a, half in Y_HOPS]
    found += [(0, a, b, way, half) for a in (0, -1, 1, 2) for way, b, half in Z_HOPS]
    if simple:
        return [t for t in found if t[4] != 1]
    found += [(1, 0, b, way, half) for way, b, half in Z_HOPS]
    return found + [(1, a, b, way, half) for b in (0, -1, 1, -2, 2, -3, 3, 4) for way, a, half in Y_HOPS]


def sender_chunk(t):
    part, a, b, way, half = t
    if way == "y+":
        return (part, {-1: 0, 2: -1}[a], b)
    if way == "y-":
        return (part, {1: 0, 2: 1}[a], b)
    if way == "z+":
        return (part, a, {-1: 0, -2: -1, -3: -2, 4: -3}[b])
    return (part, a, {1: 0, 2: 1, 3: 2, 4: 3}[b])


L_ROWS = {0: {0: (0, 32), 1: (32, 16), 2: (0, 48)}, 1: {0: (48, 32), 1: (80, 48), 2: (48, 80)}}
R_LANES = {0: {0: (0, 128), 1: (128, 128), 2: (0, 256)}, 1: {0: (256, 128), 1: (384, 128), 2: (256, 256)}}


ORDER = [
    ("own",), ("C1",), ("S", 0, 0, -1), ("S", 0, 0, 1), ("F",), ("L", 0, -1, 0), ("L", 0, 1, 0), ("L", 1, 0, -1),
    ("L", 1, 0, 1), ("L", 0, 0, -1), ("X",), ("L", 0, 0, 1), ("S", 0, 0, -2), ("S", 0, 0, 2), ("L", 1, -1, 0),
    ("L", 1, 1, 0), ("S", 0, -1, 0), ("S", 0, 1, 0), ("rows",), ("C2",), ("L", 0, 2, 0), ("L", 1, 1, -1),
    ("L", 1, -1, -1), ("L", 1, 1, 1), ("L", 1, -1, 1), ("L", 1, 2, 0), ("S", 0, 2, 0), ("L", 0, -1, -1),
    ("L", 0, -1, 1), ("L", 1, 2, -1), ("Rsum",), ("L", 0, 1, -1), ("L", 0, 1, 1), ("L", 1, 2, 1), ("L", 1, 0, -2),
    ("L", 1, 0, 2), ("L", 0, 0, -2), ("L", 0, 0, 2), ("S", 0, 0, -3), ("S", 0, 0, 3), ("S", 0, -1, -1),
    ("S", 0, -1, 1), ("S", 0, 1, -1), ("S", 0, 1, 1), ("pair", 0, 2), ("R", 0, -1, 0), ("R", 0, 1, 0),
    ("R", 1, -1, 0), ("R", 1, 1, 0), ("L", 0, 2, -1), ("L", 0, 2, 1), ("S", 0, 2, -1), ("S", 0, 2, 1), ("CX",),
    ("L", 0, -1, -2), ("L", 0, -1, 2), ("R", 0, 0, -1), ("R", 0, 0, 1), ("R", 1, 0, -1), ("R", 1, 0, 1),
    ("L", 1, -1, -2), ("L", 1, 1, -2), ("L", 0, 1, -2), ("L", 0, 1, 2), ("L", 1, -1, 2), ("L", 1, 1, 2),
    ("R", 0, 2, 0), ("R", 1, 2, 0), ("L", 1, 0, -3), ("L", 1, 0, 3), ("R", 1, -1, -1), ("R", 1, 1, -1),
    ("R", 1, -1, 1), ("R", 1, 1, 1), ("L", 0, 0, -3), ("L", 0, 0, 3), ("S", 0, 0, 4), ("pair", 0, 1), ("S", 0, -1, 2),
    ("S", 0, -1, -2), ("S", 0, 1, 2), ("S", 0, 1, -2), ("R", 0, -1, 1), ("R", 0, -1, -1), ("L", 1, 2, -2),
    ("R", 0, 1, 1), ("R", 0, 1, -1), ("pair", 0, -1), ("L", 0, 2, 2), ("L", 0, 2, -2), ("S", 0, 2, 2),
    ("S", 0, 2, -2), ("L", 1, 2, 2), ("pair", -1, 2), ("L", 0, -1, 3), ("L", 0, -1, -3), ("pair", 1, 2),
    ("R", 0, 0, 2), ("R", 0, 0, -2), ("L", 1, -1, -3), ("R", 1, 0, 2), ("R", 1, 0, -2), ("L", 1, 1, -3),
    ("pair", 2, 2), ("L", 0, 1, 3), ("L", 0, 1, -3), ("R", 0, 2, 1), ("R", 0, 2, -1), ("L", 1, -1, 3), ("L", 1, 1, 3),
    ("R", 1, 2, -1), ("R", 1, 2, 1), ("L", 1, 0, 4), ("L", 0, 0, 4), ("pair", 0, 0), ("S", 0, -1, 3),
    ("S", 0, -1, -3), ("S", 0, 1, 3), ("S", 0, 1, -3), ("R", 0, -1, 2), ("R", 0, -1, -2), ("R", 0, 1, 2),
    ("R", 0, 1, -2), ("R", 1, 1, 2), ("pair", -1, -1), ("R", 1, 1, -2), ("R", 1, -1, 2), ("R", 1, -1, -2),
    ("L", 0, 2, 3), ("L", 0, 2, -3), ("S", 0, 2, 3), ("S", 0, 2, -3), ("pair", -1, 1), ("L", 1, 2, -3),
    ("R", 0, 0, 3), ("L", 0, -1, 4), ("R", 1, 0, 3), ("R", 0, 0, -3), ("R", 1, 0, -3), ("L", 1, 2, 3),
    ("pair", 1, -1), ("R", 0, 2, 2), ("L", 0, 1, 4), ("R", 0, -1, 3), ("L", 1, -1, 4), ("R", 0, 2, -2),
    ("R", 0, 1, 3), ("S", 0, -1, 4), ("S", 0, 1, 4), ("pair", 1, 1), ("R", 0, -1, -3), ("L", 1, 1, 4),
    ("R", 0, 1, -3), ("R", 1, 2, 2), ("R", 1, 2, -2), ("pair", 2, 1), ("L", 0, 2, 4), ("S", 0, 2, 4), ("R", 0, 0, 4),
    ("pair", 2, -1), ("R", 1, -1, 3), ("R", 1, 1, 3), ("R", 1, 0, 4), ("R", 1, -1, -3), ("R", 1, 1, -3),
    ("pair", -1, 0), ("R", 0, 2, 3), ("R", 0, 2, -3), ("pair", 1, 0), ("R", 0, -1, 4), ("R", 0, 1, 4), ("L", 1, 2, 4),
    ("pair", 2, 0), ("R", 1, 2, 3), ("R", 1, -1, 4), ("R", 1, 1, 4), ("R", 1, 2, -3), ("R", 0, 2, 4), ("R", 1, 2, 4),
    ("rhs",),
]


def dot(a, b, dims):
    return lax.dot_general(a, b, (dims, ((), ())), preferred_element_type=F32)


def split2(v):
    hi = v.astype(BF16)
    return hi, (v - hi.astype(F32)).astype(BF16)


def iota(shape, axis):
    return lax.broadcasted_iota(jnp.int32, shape, axis)


def kernel(gram, inv, cross_h, down, removed, updated, rhs_out,
           gt, pt, m_ref, cross, lsrc, ssrc, lall, sall, lrow, srow, rh, rl, ch,
           c0nat, pack, yslot, fbuf, zslot, lost, hh, hl,
           g_sem, in_sem, o_sem, l_send, l_recv, s_send, s_recv, c_send, c_recv, x_send, x_recv,
           p_send, p_recv, y_send, y_recv):
    row, col, tp = lax.axis_index("row"), lax.axis_index("col"), lax.axis_index("tp")
    y, z = row // ZL, tp * ZL + lax.rem(row, ZL)
    xx, core = col // 2, lax.rem(col, 2)

    def slot_of(a, b):
        yy, zz = lax.rem(y + a + NY, NY), lax.rem(z + b + NZ, NZ)
        return yy * 8 + lax.rem(zz, ZL) * 2 + zz // ZL

    def device_of(a, b):
        yy, zz = lax.rem(y + a + NY, NY), lax.rem(z + b + NZ, NZ)
        return {"row": yy * ZL + lax.rem(zz, ZL), "col": col, "tp": zz // ZL}

    def at_col(c):
        return {"row": row, "col": c, "tp": tp}

    def peer_col(off):
        return lax.rem(xx + off, 4) * 2 + core

    to = {"y+": device_of(1, 0), "y-": device_of(-1, 0), "z+": device_of(0, 1), "z-": device_of(0, -1)}
    mine = slot_of(0, 0)

    def remote(src, dst, send, recv, dev):
        return pltpu.make_async_remote_copy(src_ref=src, dst_ref=dst, send_sem=send, recv_sem=recv, device_id=dev, device_id_type=MESH)

    loads = [pltpu.make_async_copy(gram.at[:, j, :], gt.at[j], g_sem.at[j]) for j in range(8)]
    def c0_part(first, count, c):
        return c0nat.at[pl.ds(first, count), c // 2, :, pl.ds(pl.multiple_of(512 * lax.rem(c, 2), 512), 512)]

    c0load = pltpu.make_async_copy(
        cross_h.at[pl.ds(pl.multiple_of(16 * xx, 16), 16), pl.ds(pl.multiple_of(512 * core, 512), 512)],
        c0_part(mine, 1, col).at[0], in_sem.at[0])
    m_load = pltpu.make_async_copy(inv, m_ref, in_sem.at[1])
    x_load = pltpu.make_async_copy(cross_h, cross, in_sem.at[2])

    @pl.when(y < 2)
    def _():
        c0load.start()


    @pl.when(col == 0)
    def _():
        for j in range(8):
            loads[j].start()
    m_load.start()
    x_load.start()

    barrier = pltpu.get_barrier_semaphore()
    others = [device_of(a, 0) for a in (1, 2, 3)] + [device_of(0, b) for b in range(1, 8)]
    others += [at_col(lax.rem(col + off, 8)) for off in range(1, 8)]
    for dev in others:
        pl.semaphore_signal(barrier, inc=1, device_id=dev, device_id_type=MESH)
    pl.semaphore_wait(barrier, len(others))

    class Stream:
        def __init__(self, buf, send, recv, rows, moves):
            self.buf, self.send, self.recv, self.rows, self.moves = buf, send, recv, rows, moves

        def piece(self, t, slot):
            if self.rows is None:
                return self.buf.at[slot]
            start, count = self.rows[t[0]][t[4]]
            return self.buf.at[slot, pl.ds(start, count)]

        def slot(self, a, b):
            return slot_of(a, b)

    class LaneStream(Stream):
        def piece(self, t, slot):
            start, count = self.rows[t[0]][t[4]]
            return self.buf.at[slot, :, pl.ds(start, count)]

        def slot(self, a, b):
            return lax.rem(y + a + NY, NY) * 8 + lax.rem(z + b + NZ, NZ)

    l_st = Stream(lall, l_send, l_recv, L_ROWS, plan(False))
    s_st = Stream(sall, s_send, s_recv, None, plan(True))
    r_st = LaneStream(lost, y_send, y_recv, R_LANES, plan(False))
    started = []

    def copy_of(st, i, slot):
        t = st.moves[i]
        return remote(st.piece(t, slot), st.piece(t, slot), st.send.at[i], st.recv.at[i], to[t[3]])

    def start_from(st, chunk):
        for i, t in enumerate(st.moves):
            if sender_chunk(t) == chunk:
                c = copy_of(st, i, st.slot(chunk[1], chunk[2]))
                c.start()
                started.append(c)

    def wait_for(st, chunk):
        for i, t in enumerate(st.moves):
            if t[:3] == chunk:
                copy_of(st, i, st.slot(chunk[1], chunk[2])).wait_recv()

    def many(copies):
        for c in copies:
            c.start()
        started.extend(copies)
        return copies

    def c0_z():
        return [remote(c0_part(mine, 1, col), c0_part(mine, 1, col), c_send.at[b - 1], c_recv.at[b - 1], device_of(0, b))
                for b in range(1, 8)]

    def c0_y(n):
        block = c0_part(8 * y, 8, col)
        return [remote(block, block, c_send.at[6 + a], c_recv.at[7 + n], device_of(a, 0)) for a in (1, 2, 3)]

    @pl.when(y < 2)
    def _():
        c0load.wait()
        for c in c0_z():
            c.start()

    rem = removed[...]
    flat = jnp.concatenate([rem[i:i + 1, :] for i in range(8)], axis=1)

    def first_of(base):
        less = jnp.where(rem < base, 1.0, 0.0)
        return jnp.sum(jnp.sum(less, axis=1, keepdims=True), axis=0, keepdims=True).astype(jnp.int32)

    shard = down.shape[0]
    base = mine * shard
    place = jnp.where(iota((shard, 1024), 0) == flat - base, 1.0, 0.0).astype(BF16)
    order = jnp.where(iota((128, 1024), 1) - first_of(base) == iota((128, 1024), 0), 1.0, 0.0).astype(BF16)
    pick = dot(order, place, NT).astype(BF16)
    pack[...] = dot(pick, down[...], NN).astype(BF16)
    yslot[y] = pack[...]
    ph1 = many([remote(pack, yslot.at[y], p_send.at[a - 1], p_recv.at[a - 1], device_of(a, 0)) for a in (1, 2, 3)])

    def hand_out(c):
        return [remote(lsrc.at[c], lall.at[mine], x_send.at[c - 1], x_recv.at[0], at_col(c)),
                remote(ssrc.at[c], sall.at[mine], x_send.at[7 + c - 1], x_recv.at[1], at_col(c))]

    eye = iota((64, 128), 0) == iota((64, 128), 1)

    @pl.when(col == 0)
    def _():
        for j in range(8):
            loads[j].wait()
        m_load.wait()
        for first in (4, 0):
            r0 = first * 64
            parts = [split2(gt[j, r0:r0 + 256, :]) for j in range(8)]
            hi = jnp.concatenate([p[0] for p in parts], axis=1)
            lo = jnp.concatenate([p[1] for p in parts], axis=1)
            both = jnp.concatenate([hi, lo], axis=0)
            blocks = []
            for n in range(4):
                k = 256 * (n + 1)
                d = dot(both[:, :k], m_ref[256 * n:256 * n + 256, :k], NT)
                blocks.append(d[:256] + d[256:])
            top = jnp.maximum(blocks[0], -blocks[0])
            for b in blocks[1:]:
                top = jnp.maximum(top, jnp.abs(b))
            scale = jnp.maximum(jnp.max(top, axis=1, keepdims=True), 1e-30) / 32767.0
            inverse = 1.0 / scale
            for i in range(4):
                c = first + i
                rows = slice(64 * i, 64 * i + 64)
                for n in range(4):
                    q = lax.round(blocks[n][rows] * inverse[rows], lax.RoundingMethod.TO_NEAREST_EVEN)
                    q = jnp.clip(q, -32767.0, 32767.0).astype(jnp.int32).astype(I16)
                    half, lane = n // 2, 256 * (n % 2)
                    lsrc[c, 64 * half:64 * half + 64, lane:lane + 256] = q
                lanes = jnp.sum(jnp.where(eye, jnp.broadcast_to(scale[rows], (64, 128)), 0.0), axis=0, keepdims=True)
                ssrc[c] = jnp.broadcast_to(lanes, (8, 128))
            for c in ((4, 6, 5, 7) if first == 4 else (2, 3, 1)):
                for cp in hand_out(c):
                    cp.start()

    def phase_f():
        for c in ph1:
            c.wait_recv()
        seg = jnp.concatenate([removed[pl.ds(2 * y + i, 1), :] for i in range(2)], axis=1)
        picks = []
        for yy in range(4):
            b = (yy * 8 + lax.rem(mine, 8)) * shard
            inside = (seg >= b) & (seg < b + shard)
            at = jnp.where(inside, iota((1, 256), 1) + 256 * y - first_of(b), -1)
            picks.append(jnp.where(iota((128, 256), 0) == at, 1.0, 0.0).astype(BF16))
        f = dot(jnp.concatenate(picks, axis=0), yslot[...].reshape(512, 512), TN).astype(BF16)
        for i in range(8):
            fbuf[i] = f[32 * i:32 * i + 32]
        zslot[z] = fbuf[z]
        return many([remote(fbuf.at[lax.rem(z + b, 8)], zslot.at[z], p_send.at[3 + b - 1], p_recv.at[3 + b - 1], device_of(0, b))
                     for b in range(1, 8)])

    def phase_r(ph2):
        for c in ph2:
            c.wait_recv()
        total = zslot[0].astype(F32)
        for i in range(1, 8):
            total = total + zslot[i].astype(F32)
        lost[y * 8 + z] = total.astype(BF16)
        for part in (0, 1):
            start_from(r_st, (part, 0, 0))

    def x_peers(n, src, dst):
        return many([remote(src, dst.at[col], x_send.at[14 + 7 * n + off - 1], x_recv.at[2 + 7 * n + off - 1], at_col(peer_col(off)))
                     for off in range(1, 4)])

    def to_sibling(n, off, src, dst, slot):
        return many([remote(src, dst.at[slot], x_send.at[14 + 7 * n + 3 + off], x_recv.at[2 + 7 * n + 3 + off], at_col(col + 1 - 2 * core))])

    state = {}

    def own_rows():
        @pl.when(col == 0)
        def _():
            lall[mine] = lsrc[0]
            sall[mine] = ssrc[0]

        @pl.when(col != 0)
        def _():
            for k, dst in enumerate((lall, sall)):
                remote(dst.at[mine], dst.at[mine], x_send.at[0], x_recv.at[k], to["y+"]).wait_recv()
        for part in (0, 1):
            start_from(l_st, (part, 0, 0))
        start_from(s_st, (0, 0, 0))
        lrow[col] = lall[mine]
        srow[col] = sall[mine]
        state["xl"] = x_peers(0, lrow.at[col], lrow)
        state["xs"] = x_peers(1, srow.at[col], srow)
        state["sl"] = to_sibling(0, 0, lrow.at[col], lrow, col)
        state["ss"] = to_sibling(1, 0, srow.at[col], srow, col)

    def forward_rows(n, key, skey, buf):
        for off in range(1, 4):
            state[key][off - 1].wait_recv()
            c = lax.rem(xx - off + 4, 4) * 2 + core
            state[skey] += to_sibling(n, off, buf.at[c], buf, c)

    def dequant(q_ref, s_ref, slot):
        s = jnp.sum(jnp.where(eye, jnp.broadcast_to(s_ref[slot, 0:1, :], (64, 128)), 0.0), axis=1, keepdims=True)
        v = jnp.concatenate([q_ref[slot, 0:64, :], q_ref[slot, 64:128, :]], axis=1)
        return split2(v.astype(jnp.int32).astype(F32) * s)

    def rows_ready():
        for k in ("sl", "ss"):
            for c in state[k]:
                c.wait_recv()

        def body(c, _):
            hi, lo = dequant(lrow, srow, c)
            at = pl.ds(pl.multiple_of(64 * c, 64), 64)
            rh[at, :] = hi
            rl[at, :] = lo
            return 0
        lax.fori_loop(0, 8, body, 0)

    outs = []

    def columns(n, a, b):
        yy, zl = lax.rem(y + a + NY, NY), lax.rem(z + b + NZ, ZL)
        j = yy * 4 + zl
        for i in range(2):
            hi, lo = dequant(lall, sall, 2 * j + i)
            ch[64 * i:64 * i + 64, :] = hi
            ch[128 + 64 * i:192 + 64 * i, :] = lo
        p = dot(rh[...], ch[...], NT)
        p = p[:, :128] + p[:, 128:] + dot(rl[...], ch[:128], NT)
        pt[j] = p
        cp = pltpu.make_async_copy(pt.at[j], updated.at[:, j, :], o_sem.at[n])
        cp.start()
        outs.append(cp)

    def right_side():
        for c in state["sc"]:
            c.wait_recv()
        x_load.wait()
        r_hi, r_lo = split2(dot(c0nat[...].reshape(1024, 1024), lost[...].reshape(1024, 512), NN))
        for n in range(4):
            k = 256 * (n + 1)
            mm = m_ref[256 * n:256 * n + 256, :k]
            hi, lo = split2(dot(mm, r_hi[:k], NN) + dot(mm, r_lo[:k], NN))
            hh[256 * n:256 * n + 256, :] = hi
            hl[256 * n:256 * n + 256, :] = lo
        rhs = dot(cross[...], lost[...].reshape(1024, 512), NN)
        rhs_out[...] = rhs - (dot(rh[...], hh[...], NN) + dot(rh[...], hl[...], NN) + dot(rl[...], hh[...], NN))

    def c0_across():
        @pl.when(y < 2)
        def _():
            for c in c0_z():
                c.wait_recv()

        for n in range(2):
            @pl.when(y == n)
            def _():
                for c in c0_y(n):
                    c.start()

    def c0_done():
        for n in range(2):
            @pl.when(y != n)
            def _():
                block = c0_part(8 * n, 8, col)
                remote(block, block, c_send.at[0], c_recv.at[7 + n], to["y+"]).wait_recv()
        own = c0_part(0, 16, col)
        state["xc"] = many([remote(own, own, x_send.at[28 + off - 1], x_recv.at[16 + off - 1], at_col(peer_col(off))) for off in range(1, 4)])
        state["sc"] = many([remote(own, own, x_send.at[31], x_recv.at[19], at_col(col + 1 - 2 * core))])

    def c0_forward():
        for off in range(1, 4):
            state["xc"][off - 1].wait_recv()
            block = c0_part(0, 16, lax.rem(xx - off + 4, 4) * 2 + core)
            state["sc"] += many([remote(block, block, x_send.at[31 + off], x_recv.at[19 + off], at_col(col + 1 - 2 * core))])

    def loaded():
        @pl.when(col != 0)
        def _():
            m_load.wait()

    streams = {"L": l_st, "R": r_st, "S": s_st}
    steps = {
        "own": own_rows,
        "F": lambda: state.update(ph2=phase_f()),
        "Rsum": lambda: phase_r(state["ph2"]),
        "C1": c0_across,
        "C2": c0_done,
        "CX": c0_forward,
        "X": lambda: (forward_rows(1, "xs", "ss", srow), forward_rows(0, "xl", "sl", lrow)),
        "rows": lambda: (loaded(), rows_ready()),
        "rhs": right_side,
    }
    pairs = 0
    for event in ORDER:
        if event[0] in streams:
            wait_for(streams[event[0]], event[1:])
            start_from(streams[event[0]], event[1:])
        elif event[0] == "pair":
            columns(pairs, event[1], event[2])
            pairs += 1
        else:
            steps[event[0]]()
    for c in started:
        c.wait_send()
    for c in outs:
        c.wait()

    @pl.when(y < 2)
    def _():
        for c in c0_z() + c0_y(0):
            c.wait_send()

    @pl.when(col == 0)
    def _():
        for c in range(1, 8):
            for cp in hand_out(c):
                cp.wait_send()


def per_device(gram, inv_factor, cross_gram, down_rows, removed):
    vm = pl.BlockSpec(memory_space=pltpu.VMEM)
    hbm = pl.BlockSpec(memory_space=pl.ANY)
    dma = pltpu.SemaphoreType.DMA
    big, small = len(plan(False)), len(plan(True))
    v = pltpu.VMEM
    updated, rhs = pl.pallas_call(
        kernel,
        out_shape=[jax.ShapeDtypeStruct((512, 16, 128), F32), jax.ShapeDtypeStruct((512, 512), F32)],
        in_specs=[hbm, hbm, hbm, vm, vm],
        out_specs=[hbm, vm],
        scratch_shapes=[
            v((8, 512, 128), F32), v((16, 512, 128), F32), v((1024, 1024), BF16), v((512, 1024), BF16),
            v((8, 128, 512), I16), v((8, 8, 128), F32), v((32, 128, 512), I16), v((32, 8, 128), F32),
            v((8, 128, 512), I16), v((8, 8, 128), F32), v((512, 1024), BF16), v((512, 1024), BF16),
            v((256, 1024), BF16),
            v((16, 4, 16, 1024), BF16), v((128, 512), BF16), v((4, 128, 512), BF16),
            v((8, 32, 512), BF16), v((8, 32, 512), BF16), v((32, 32, 512), BF16),
            v((1024, 512), BF16), v((1024, 512), BF16),
            dma((8,)), dma((3,)), dma((16,)), dma((big,)), dma((big,)), dma((small,)), dma((small,)),
            dma((10,)), dma((9,)), dma((35,)), dma((23,)), dma((10,)), dma((10,)), dma((big,)), dma((big,)),
        ],
        compiler_params=pltpu.CompilerParams(collective_id=0, has_side_effects=True, vmem_limit_bytes=56 << 20),
    )(gram.reshape(512, 16, 128), inv_factor, cross_gram.reshape(512, 1024), down_rows, removed.reshape(8, 128))
    updated = gram.reshape(512, 16, 128) - updated
    return (updated.reshape(gram.shape), rhs.reshape(8, 1, 64, 512))


def solution(mesh):
    return jax.shard_map(
        per_device,
        mesh=mesh,
        in_specs=(
            P(None, "row", "tp", None, "col", None),
            P(),
            P(None, "row", "tp", None),
            P(("row", "tp"), "col"),
            P(),
        ),
        out_specs=(P(None, "row", "tp", None, "col", None), P(None, "row", "tp", "col")),
        check_vma=False,
    )
```

```python
import jax
import jax.numpy as jnp
from jax import lax
from jax.experimental import pallas as pl
from jax.experimental.pallas import tpu as pltpu
from jax.sharding import PartitionSpec as P

NY, NZ, ZL = 4, 8, 4
MESH = pl.DeviceIdType.MESH
F32, BF16, I16 = jnp.float32, jnp.bfloat16, jnp.int16
NT, NN, TN = ((1,), (1,)), ((1,), (0,)), ((0,), (0,))
Z_HOPS = [("z+", -1, 2), ("z-", 1, 2), ("z+", -2, 2), ("z-", 2, 2), ("z+", -3, 2), ("z-", 3, 2), ("z+", 4, 0), ("z-", 4, 1)]
Y_HOPS = [("y+", -1, 2), ("y-", 1, 2), ("y+", 2, 0), ("y-", 2, 1)]


def plan(simple):
    found = [(0, a, 0, way, half) for way, a, half in Y_HOPS]
    found += [(0, a, b, way, half) for a in (0, -1, 1, 2) for way, b, half in Z_HOPS]
    if simple:
        return [t for t in found if t[4] != 1]
    found += [(1, 0, b, way, half) for way, b, half in Z_HOPS]
    return found + [(1, a, b, way, half) for b in (0, -1, 1, -2, 2, -3, 3, 4) for way, a, half in Y_HOPS]


def sender_chunk(t):
    part, a, b, way, half = t
    if way == "y+":
        return (part, {-1: 0, 2: -1}[a], b)
    if way == "y-":
        return (part, {1: 0, 2: 1}[a], b)
    if way == "z+":
        return (part, a, {-1: 0, -2: -1, -3: -2, 4: -3}[b])
    return (part, a, {1: 0, 2: 1, 3: 2, 4: 3}[b])


L_ROWS = {0: {0: (0, 32), 1: (32, 16), 2: (0, 48)}, 1: {0: (48, 32), 1: (80, 48), 2: (48, 80)}}
R_LANES = {0: {0: (0, 128), 1: (128, 128), 2: (0, 256)}, 1: {0: (256, 128), 1: (384, 128), 2: (256, 256)}}


ORDER = [
    ("own",), ("S", 0, 0, -1), ("S", 0, 0, 1), ("C1",), ("L", 1, 0, -1), ("L", 1, 0, 1), ("F",), ("L", 0, 0, -1),
    ("X",), ("L", 0, 0, 1), ("S", 0, 0, -2), ("L", 0, -1, 0), ("S", 0, 0, 2), ("L", 0, 1, 0), ("L", 1, -1, 0),
    ("L", 1, 1, 0), ("S", 0, -1, 0), ("S", 0, 1, 0), ("rows",), ("L", 1, 0, -2), ("L", 1, 0, 2), ("C2",),
    ("L", 1, -1, -1), ("L", 1, 1, -1), ("L", 1, -1, 1), ("L", 1, 1, 1), ("L", 0, 2, 0), ("L", 1, 2, 0),
    ("S", 0, 2, 0), ("L", 0, 0, -2), ("S", 0, 0, -3), ("L", 0, 0, 2), ("pair", 0, 2), ("Rsum",), ("L", 0, -1, -1),
    ("L", 0, -1, 1), ("L", 1, 1, -2), ("S", 0, 0, 3), ("L", 1, -1, -2), ("L", 0, 1, -1), ("S", 0, -1, -1),
    ("S", 0, 1, -1), ("L", 0, 1, 1), ("S", 0, -1, 1), ("S", 0, 1, 1), ("L", 1, 1, 2), ("L", 1, -1, 2),
    ("L", 1, 2, -1), ("L", 1, 0, -3), ("L", 1, 0, 3), ("CX",), ("R", 0, -1, 0), ("L", 1, 2, 1), ("L", 0, 2, -1),
    ("R", 1, -1, 0), ("S", 0, 2, -1), ("L", 0, 2, 1), ("S", 0, 2, 1), ("R", 0, 1, 0), ("R", 1, 1, 0), ("L", 0, 0, -3),
    ("pair", 0, 1), ("S", 0, 0, 4), ("L", 0, 0, 3), ("R", 0, 0, -1), ("R", 0, 0, 1), ("L", 1, 2, -2), ("R", 1, 0, -1),
    ("R", 1, 0, 1), ("pair", 0, -1), ("L", 1, 2, 2), ("L", 0, -1, -2), ("L", 0, -1, 2), ("L", 1, -1, -3),
    ("L", 0, 1, -2), ("S", 0, -1, -2), ("L", 0, 1, 2), ("S", 0, 1, -2), ("S", 0, -1, 2), ("S", 0, 1, 2),
    ("pair", -1, 2), ("L", 1, 1, -3), ("R", 0, -1, -1), ("pair", 1, 2), ("L", 1, 0, 4), ("L", 1, -1, 3),
    ("R", 0, -1, 1), ("CW",), ("R", 1, -1, -1), ("L", 1, 1, 3), ("L", 0, 2, -2), ("S", 0, 2, -2), ("R", 1, -1, 1),
    ("R", 0, 2, 0), ("R", 1, 2, 0), ("R", 0, 1, -1), ("L", 0, 2, 2), ("S", 0, 2, 2), ("pair", 2, 2), ("R", 1, 1, -1),
    ("R", 0, 1, 1), ("R", 1, 1, 1), ("L", 0, 0, 4), ("R", 0, 0, -2), ("R", 0, 0, 2), ("pair", 0, 0), ("R", 1, 0, -2),
    ("R", 1, 0, 2), ("L", 1, 2, -3), ("L", 0, -1, -3), ("L", 0, -1, 3), ("L", 0, 1, -3), ("S", 0, -1, -3),
    ("L", 0, 1, 3), ("S", 0, 1, -3), ("S", 0, -1, 3), ("S", 0, 1, 3), ("pair", -1, 1), ("L", 1, -1, 4),
    ("R", 0, -1, -2), ("R", 0, -1, 2), ("L", 1, 1, 4), ("R", 0, 2, 1), ("pair", 1, 1), ("L", 0, 2, -3),
    ("S", 0, 2, -3), ("L", 1, 2, 3), ("R", 1, 2, -1), ("R", 1, -1, -2), ("R", 0, 2, -1), ("L", 0, 2, 3),
    ("R", 1, 2, 1), ("S", 0, 2, 3), ("R", 1, -1, 2), ("R", 0, 1, -2), ("R", 1, 1, -2), ("R", 0, 1, 2),
    ("pair", -1, -1), ("R", 0, 0, -3), ("R", 1, 1, 2), ("R", 0, 0, 3), ("R", 1, 0, -3), ("R", 1, 0, 3),
    ("L", 0, -1, 4), ("pair", 1, -1), ("R", 0, -1, 3), ("L", 0, 1, 4), ("S", 0, -1, 4), ("S", 0, 1, 4),
    ("R", 0, 2, 2), ("pair", 2, 1), ("R", 0, -1, -3), ("L", 1, 2, 4), ("R", 1, 2, -2), ("L", 0, 2, 4),
    ("pair", 2, -1), ("S", 0, 2, 4), ("R", 0, 1, 3), ("R", 0, 2, -2), ("R", 0, 1, -3), ("R", 1, 2, 2), ("R", 0, 0, 4),
    ("pair", -1, 0), ("R", 1, 0, 4), ("R", 1, -1, -3), ("R", 1, 1, -3), ("R", 1, -1, 3), ("R", 1, 1, 3),
    ("pair", 1, 0), ("R", 0, 2, 3), ("pair", 2, 0), ("R", 0, -1, 4), ("R", 0, 2, -3), ("R", 0, 1, 4), ("R", 1, -1, 4),
    ("R", 1, 1, 4), ("R", 1, 2, -3), ("R", 1, 2, 3), ("R", 0, 2, 4), ("rhs", 0), ("R", 1, 2, 4), ("rhs", 1),
]


def dot(a, b, dims):
    return lax.dot_general(a, b, (dims, ((), ())), preferred_element_type=F32)


def split2(v):
    hi = v.astype(BF16)
    return hi, (v - hi.astype(F32)).astype(BF16)


def iota(shape, axis):
    return lax.broadcasted_iota(jnp.int32, shape, axis)


def kernel(gram, inv, cross_h, down_h, removed_h, updated, rhs_out,
           down, removed,
           gt, pt, m_ref, cross, lsrc, ssrc, lall, sall, lrow, srow, rh, rl, ch,
           c0nat, pack, yslot, fbuf, zslot, lost, hh, hl,
           g_sem, in_sem, o_sem, l_send, l_recv, s_send, s_recv, c_send, c_recv, x_send, x_recv,
           p_send, p_recv, y_send, y_recv):
    row, col, tp = lax.axis_index("row"), lax.axis_index("col"), lax.axis_index("tp")
    y, z = row // ZL, tp * ZL + lax.rem(row, ZL)
    xx, core = col // 2, lax.rem(col, 2)

    def slot_of(a, b):
        yy, zz = lax.rem(y + a + NY, NY), lax.rem(z + b + NZ, NZ)
        return yy * 8 + lax.rem(zz, ZL) * 2 + zz // ZL

    def device_of(a, b):
        yy, zz = lax.rem(y + a + NY, NY), lax.rem(z + b + NZ, NZ)
        return {"row": yy * ZL + lax.rem(zz, ZL), "col": col, "tp": zz // ZL}

    def at_col(c):
        return {"row": row, "col": c, "tp": tp}

    def peer_col(off):
        return lax.rem(xx + off, 4) * 2 + core

    to = {"y+": device_of(1, 0), "y-": device_of(-1, 0), "z+": device_of(0, 1), "z-": device_of(0, -1)}
    mine = slot_of(0, 0)

    def remote(src, dst, send, recv, dev):
        return pltpu.make_async_remote_copy(src_ref=src, dst_ref=dst, send_sem=send, recv_sem=recv, device_id=dev, device_id_type=MESH)

    loads = [pltpu.make_async_copy(gram.at[:, j, :], gt.at[j], g_sem.at[j]) for j in range(8)]
    def c0_part(first, count, c):
        return c0nat.at[pl.ds(first, count), c // 2, :, pl.ds(pl.multiple_of(512 * lax.rem(c, 2), 512), 512)]

    c0load = pltpu.make_async_copy(
        cross_h.at[pl.ds(pl.multiple_of(16 * xx, 16), 16), pl.ds(pl.multiple_of(512 * core, 512), 512)],
        c0_part(mine, 1, col).at[0], in_sem.at[0])
    m_load = pltpu.make_async_copy(inv, m_ref, in_sem.at[1])
    x_load = pltpu.make_async_copy(cross_h, cross, in_sem.at[2])

    @pl.when(y < 2)
    def _():
        c0load.start()


    @pl.when(col == 0)
    def _():
        for j in range(8):
            loads[j].start()
    d_load = pltpu.make_async_copy(down_h, down, in_sem.at[3])
    i_load = pltpu.make_async_copy(removed_h, removed, in_sem.at[4])
    i_load.start()
    m_load.start()
    d_load.start()
    x_load.start()

    barrier = pltpu.get_barrier_semaphore()
    others = [device_of(a, 0) for a in (1, 2, 3)] + [device_of(0, b) for b in range(1, 8)]
    others += [at_col(lax.rem(col + off, 8)) for off in range(1, 8)]
    for dev in others:
        pl.semaphore_signal(barrier, inc=1, device_id=dev, device_id_type=MESH)

    class Stream:
        def __init__(self, buf, send, recv, rows, moves):
            self.buf, self.send, self.recv, self.rows, self.moves = buf, send, recv, rows, moves

        def piece(self, t, slot):
            if self.rows is None:
                return self.buf.at[slot]
            start, count = self.rows[t[0]][t[4]]
            return self.buf.at[slot, pl.ds(start, count)]

        def slot(self, a, b):
            return slot_of(a, b)

    class LaneStream(Stream):
        def piece(self, t, slot):
            start, count = self.rows[t[0]][t[4]]
            return self.buf.at[slot, :, pl.ds(start, count)]

        def slot(self, a, b):
            return lax.rem(y + a + NY, NY) * 8 + lax.rem(z + b + NZ, NZ)

    l_st = Stream(lall, l_send, l_recv, L_ROWS, plan(False))
    s_st = Stream(sall, s_send, s_recv, None, plan(True))
    r_st = LaneStream(lost, y_send, y_recv, R_LANES, plan(False))
    started = []

    def copy_of(st, i, slot):
        t = st.moves[i]
        return remote(st.piece(t, slot), st.piece(t, slot), st.send.at[i], st.recv.at[i], to[t[3]])

    def start_from(st, chunk):
        for i, t in enumerate(st.moves):
            if sender_chunk(t) == chunk:
                c = copy_of(st, i, st.slot(chunk[1], chunk[2]))
                c.start()
                started.append(c)

    def wait_for(st, chunk):
        for i, t in enumerate(st.moves):
            if t[:3] == chunk:
                copy_of(st, i, st.slot(chunk[1], chunk[2])).wait_recv()

    def many(copies):
        for c in copies:
            c.start()
        started.extend(copies)
        return copies

    def c0_z():
        return [remote(c0_part(mine, 1, col), c0_part(mine, 1, col), c_send.at[b - 1], c_recv.at[b - 1], device_of(0, b))
                for b in range(1, 8)]

    def c0_y(n):
        block = c0_part(8 * y, 8, col)
        return [remote(block, block, c_send.at[6 + a], c_recv.at[7 + n], device_of(a, 0)) for a in (1, 2, 3)]

    def hand_out(c):
        return [remote(lsrc.at[c], lall.at[mine], x_send.at[c - 1], x_recv.at[0], at_col(c)),
                remote(ssrc.at[c], sall.at[mine], x_send.at[7 + c - 1], x_recv.at[1], at_col(c))]

    eye = iota((64, 128), 0) == iota((64, 128), 1)

    def factor_rows(first):
        r0 = first * 64
        parts = [split2(gt[j, r0:r0 + 128, :]) for j in range(8)]
        hi = jnp.concatenate([p[0] for p in parts], axis=1)
        lo = jnp.concatenate([p[1] for p in parts], axis=1)
        both = jnp.concatenate([hi, lo], axis=0)
        blocks = []
        for n in range(4):
            k = 256 * (n + 1)
            d = dot(both[:, :k], m_ref[256 * n:256 * n + 256, :k], NT)
            blocks.append(d[:128] + d[128:])
        top = jnp.maximum(blocks[0], -blocks[0])
        for b in blocks[1:]:
            top = jnp.maximum(top, jnp.abs(b))
        scale = jnp.maximum(jnp.max(top, axis=1, keepdims=True), 1e-30) / 32767.0
        inverse = 1.0 / scale
        for i in range(2):
            c = first + i
            rows = slice(64 * i, 64 * i + 64)
            for n in range(4):
                q = lax.round(blocks[n][rows] * inverse[rows], lax.RoundingMethod.TO_NEAREST_EVEN)
                q = jnp.clip(q, -32767.0, 32767.0).astype(jnp.int32).astype(I16)
                half, lane = n // 2, 256 * (n % 2)
                lsrc[c, 64 * half:64 * half + 64, lane:lane + 256] = q
            lanes = jnp.sum(jnp.where(eye, jnp.broadcast_to(scale[rows], (64, 128)), 0.0), axis=0, keepdims=True)
            ssrc[c] = jnp.broadcast_to(lanes, (8, 128))

    @pl.when(col == 0)
    def _():
        for j in range(8):
            loads[j].wait()
        m_load.wait()
        factor_rows(6)
        factor_rows(4)

    i_load.wait()
    rem = removed[...]
    flat = jnp.concatenate([rem[i:i + 1, :] for i in range(8)], axis=1)

    def first_of(base):
        less = jnp.where(rem < base, 1.0, 0.0)
        return jnp.sum(jnp.sum(less, axis=1, keepdims=True), axis=0, keepdims=True).astype(jnp.int32)

    shard = down.shape[0]
    base = mine * shard
    place = jnp.where(iota((shard, 1024), 0) == flat - base, 1.0, 0.0).astype(BF16)
    order = jnp.where(iota((128, 1024), 1) - first_of(base) == iota((128, 1024), 0), 1.0, 0.0).astype(BF16)
    pick = dot(order, place, NT).astype(BF16)
    d_load.wait()
    pack[...] = dot(pick, down[...], NN).astype(BF16)
    pl.semaphore_wait(barrier, len(others))

    @pl.when(col == 0)
    def _():
        for c in (6, 4, 7, 5):
            for cp in hand_out(c):
                cp.start()

    @pl.when(y < 2)
    def _():
        c0load.wait()
        for c in c0_z():
            c.start()

    yslot[y] = pack[...]
    ph1 = many([remote(pack, yslot.at[y], p_send.at[a - 1], p_recv.at[a - 1], device_of(a, 0)) for a in (1, 2, 3)])

    @pl.when(col == 0)
    def _():
        for first in (2, 0):
            factor_rows(first)
            for c in range(max(first, 1), first + 2):
                for cp in hand_out(c):
                    cp.start()

    def phase_f():
        for c in ph1:
            c.wait_recv()
        seg = jnp.concatenate([removed[pl.ds(2 * y + i, 1), :] for i in range(2)], axis=1)
        picks = []
        for yy in range(4):
            b = (yy * 8 + lax.rem(mine, 8)) * shard
            inside = (seg >= b) & (seg < b + shard)
            at = jnp.where(inside, iota((1, 256), 1) + 256 * y - first_of(b), -1)
            picks.append(jnp.where(iota((128, 256), 0) == at, 1.0, 0.0).astype(BF16))
        f = dot(jnp.concatenate(picks, axis=0), yslot[...].reshape(512, 512), TN).astype(BF16)
        for i in range(8):
            fbuf[i] = f[32 * i:32 * i + 32]
        zslot[z] = fbuf[z]
        return many([remote(fbuf.at[lax.rem(z + b, 8)], zslot.at[z], p_send.at[3 + b - 1], p_recv.at[3 + b - 1], device_of(0, b))
                     for b in range(1, 8)])

    def phase_r(ph2):
        for c in ph2:
            c.wait_recv()
        total = zslot[0].astype(F32)
        for i in range(1, 8):
            total = total + zslot[i].astype(F32)
        lost[y * 8 + z] = total.astype(BF16)
        for part in (0, 1):
            start_from(r_st, (part, 0, 0))

    def x_peers(n, src, dst):
        return many([remote(src, dst.at[col], x_send.at[14 + 7 * n + off - 1], x_recv.at[2 + 7 * n + off - 1], at_col(peer_col(off)))
                     for off in range(1, 4)])

    def to_sibling(n, off, src, dst, slot):
        return many([remote(src, dst.at[slot], x_send.at[14 + 7 * n + 3 + off], x_recv.at[2 + 7 * n + 3 + off], at_col(col + 1 - 2 * core))])

    state = {}

    def own_rows():
        @pl.when(col == 0)
        def _():
            lall[mine] = lsrc[0]
            sall[mine] = ssrc[0]

        @pl.when(col != 0)
        def _():
            for k, dst in enumerate((lall, sall)):
                remote(dst.at[mine], dst.at[mine], x_send.at[0], x_recv.at[k], to["y+"]).wait_recv()
        for part in (0, 1):
            start_from(l_st, (part, 0, 0))
        start_from(s_st, (0, 0, 0))
        lrow[col] = lall[mine]
        srow[col] = sall[mine]
        state["xl"] = x_peers(0, lrow.at[col], lrow)
        state["xs"] = x_peers(1, srow.at[col], srow)
        state["sl"] = to_sibling(0, 0, lrow.at[col], lrow, col)
        state["ss"] = to_sibling(1, 0, srow.at[col], srow, col)

    def forward_rows(n, key, skey, buf):
        for off in range(1, 4):
            state[key][off - 1].wait_recv()
            c = lax.rem(xx - off + 4, 4) * 2 + core
            state[skey] += to_sibling(n, off, buf.at[c], buf, c)

    def dequant(q_ref, s_ref, slot):
        s = jnp.sum(jnp.where(eye, jnp.broadcast_to(s_ref[slot, 0:1, :], (64, 128)), 0.0), axis=1, keepdims=True)
        v = jnp.concatenate([q_ref[slot, 0:64, :], q_ref[slot, 64:128, :]], axis=1)
        return split2(v.astype(jnp.int32).astype(F32) * s)

    def rows_ready():
        for k in ("sl", "ss"):
            for c in state[k]:
                c.wait_recv()

        def body(c, _):
            hi, lo = dequant(lrow, srow, c)
            at = pl.ds(pl.multiple_of(64 * c, 64), 64)
            rh[at, :] = hi
            rl[at, :] = lo
            return 0
        lax.fori_loop(0, 8, body, 0)

    outs = []

    def columns(n, a, b):
        yy, zl = lax.rem(y + a + NY, NY), lax.rem(z + b + NZ, ZL)
        j = yy * 4 + zl
        for i in range(2):
            hi, lo = dequant(lall, sall, 2 * j + i)
            ch[64 * i:64 * i + 64, :] = hi
            ch[128 + 64 * i:192 + 64 * i, :] = lo
        p = dot(rh[...], ch[...], NT)
        p = p[:, :128] + p[:, 128:] + dot(rl[...], ch[:128], NT)
        pt[j] = p
        cp = pltpu.make_async_copy(pt.at[j], updated.at[:, j, :], o_sem.at[n])
        cp.start()
        outs.append(cp)

    def right_side(part):
        lanes = slice(256 * part, 256 * part + 256)
        r_hi, r_lo = split2(dot(c0nat[...].reshape(1024, 1024), lost[:, :, lanes].reshape(1024, 256), NN))
        for n in range(4):
            k = 256 * (n + 1)
            mm = m_ref[256 * n:256 * n + 256, :k]
            hi, lo = split2(dot(mm, r_hi[:k], NN) + dot(mm, r_lo[:k], NN))
            hh[256 * n:256 * n + 256, :] = hi
            hl[256 * n:256 * n + 256, :] = lo
        rhs = dot(cross[...], lost[:, :, lanes].reshape(1024, 256), NN)
        rhs_out[:, lanes] = rhs - (dot(rh[...], hh[...], NN) + dot(rh[...], hl[...], NN) + dot(rl[...], hh[...], NN))

    def c0_across():
        @pl.when(y < 2)
        def _():
            for c in c0_z():
                c.wait_recv()

        for n in range(2):
            @pl.when(y == n)
            def _():
                for c in c0_y(n):
                    c.start()

    def c0_done():
        for n in range(2):
            @pl.when(y != n)
            def _():
                block = c0_part(8 * n, 8, col)
                remote(block, block, c_send.at[0], c_recv.at[7 + n], to["y+"]).wait_recv()
        own = c0_part(0, 16, col)
        state["xc"] = many([remote(own, own, x_send.at[28 + off - 1], x_recv.at[16 + off - 1], at_col(peer_col(off))) for off in range(1, 4)])
        state["sc"] = many([remote(own, own, x_send.at[31], x_recv.at[19], at_col(col + 1 - 2 * core))])

    def c0_forward():
        for off in range(1, 4):
            state["xc"][off - 1].wait_recv()
            block = c0_part(0, 16, lax.rem(xx - off + 4, 4) * 2 + core)
            state["sc"] += many([remote(block, block, x_send.at[31 + off], x_recv.at[19 + off], at_col(col + 1 - 2 * core))])

    def loaded():
        @pl.when(col != 0)
        def _():
            m_load.wait()

    streams = {"L": l_st, "R": r_st, "S": s_st}
    steps = {
        "own": own_rows,
        "F": lambda: state.update(ph2=phase_f()),
        "Rsum": lambda: phase_r(state["ph2"]),
        "C1": c0_across,
        "C2": c0_done,
        "CX": c0_forward,
        "CW": lambda: ([c.wait_recv() for c in state["sc"]], x_load.wait()),
        "X": lambda: (forward_rows(1, "xs", "ss", srow), forward_rows(0, "xl", "sl", lrow)),
        "rows": lambda: (loaded(), rows_ready()),
            }
    pairs = 0
    for event in ORDER:
        if event[0] in streams:
            wait_for(streams[event[0]], event[1:])
            start_from(streams[event[0]], event[1:])
        elif event[0] == "rhs":
            right_side(event[1])
        elif event[0] == "pair":
            columns(pairs, event[1], event[2])
            pairs += 1
        else:
            steps[event[0]]()
    for c in started:
        c.wait_send()
    for c in outs:
        c.wait()

    @pl.when(y < 2)
    def _():
        for c in c0_z() + c0_y(0):
            c.wait_send()

    @pl.when(col == 0)
    def _():
        for c in range(1, 8):
            for cp in hand_out(c):
                cp.wait_send()


def per_device(gram, inv_factor, cross_gram, down_rows, removed):
    vm = pl.BlockSpec(memory_space=pltpu.VMEM)
    hbm = pl.BlockSpec(memory_space=pl.ANY)
    dma = pltpu.SemaphoreType.DMA
    big, small = len(plan(False)), len(plan(True))
    v = pltpu.VMEM
    updated, rhs = pl.pallas_call(
        kernel,
        out_shape=[jax.ShapeDtypeStruct((512, 16, 128), F32), jax.ShapeDtypeStruct((512, 512), F32)],
        in_specs=[hbm] * 5,
        out_specs=[hbm, vm],
        scratch_shapes=[
            v(down_rows.shape, BF16), v((8, 128), jnp.int32), v((8, 512, 128), F32), v((16, 512, 128), F32), v((1024, 1024), BF16), v((512, 1024), BF16),
            v((8, 128, 512), I16), v((8, 8, 128), F32), v((32, 128, 512), I16), v((32, 8, 128), F32),
            v((8, 128, 512), I16), v((8, 8, 128), F32), v((512, 1024), BF16), v((512, 1024), BF16),
            v((256, 1024), BF16),
            v((16, 4, 16, 1024), BF16), v((128, 512), BF16), v((4, 128, 512), BF16),
            v((8, 32, 512), BF16), v((8, 32, 512), BF16), v((32, 32, 512), BF16),
            v((1024, 256), BF16), v((1024, 256), BF16),
            dma((8,)), dma((5,)), dma((16,)), dma((big,)), dma((big,)), dma((small,)), dma((small,)),
            dma((10,)), dma((9,)), dma((35,)), dma((23,)), dma((10,)), dma((10,)), dma((big,)), dma((big,)),
        ],
        cost_estimate=pl.CostEstimate(flops=15_000_000_000, bytes_accessed=13_000_000, transcendentals=0),
        compiler_params=pltpu.CompilerParams(collective_id=0, has_side_effects=True, vmem_limit_bytes=56 << 20),
    )(gram.reshape(512, 16, 128), inv_factor, cross_gram.reshape(512, 1024), down_rows, removed.reshape(8, 128))
    updated = gram.reshape(512, 16, 128) - updated
    return (updated.reshape(gram.shape), rhs.reshape(8, 1, 64, 512))


def solution(mesh):
    return jax.shard_map(
        per_device,
        mesh=mesh,
        in_specs=(
            P(None, "row", "tp", None, "col", None),
            P(),
            P(None, "row", "tp", None),
            P(("row", "tp"), "col"),
            P(),
        ),
        out_specs=(P(None, "row", "tp", None, "col", None), P(None, "row", "tp", "col")),
        check_vma=False,
    )
```

```python
import jax
import jax.numpy as jnp
from jax import lax
from jax.experimental import pallas as pl
from jax.experimental.pallas import tpu as pltpu
from jax.sharding import PartitionSpec as P

NY, NZ, ZL = 4, 8, 4
MESH = pl.DeviceIdType.MESH
F32, BF16, I16 = jnp.float32, jnp.bfloat16, jnp.int16
NT, NN, TN = ((1,), (1,)), ((1,), (0,)), ((0,), (0,))
Z_HOPS = [("z+", -1, 2), ("z-", 1, 2), ("z+", -2, 2), ("z-", 2, 2), ("z+", -3, 2), ("z-", 3, 2), ("z+", 4, 0), ("z-", 4, 1)]
Y_HOPS = [("y+", -1, 2), ("y-", 1, 2), ("y+", 2, 0), ("y-", 2, 1)]


def plan(simple):
    found = [(0, a, 0, way, half) for way, a, half in Y_HOPS]
    found += [(0, a, b, way, half) for a in (0, -1, 1, 2) for way, b, half in Z_HOPS]
    if simple:
        return [t for t in found if t[4] != 1]
    found += [(1, 0, b, way, half) for way, b, half in Z_HOPS]
    return found + [(1, a, b, way, half) for b in (0, -1, 1, -2, 2, -3, 3, 4) for way, a, half in Y_HOPS]


def sender_chunk(t):
    part, a, b, way, half = t
    if way == "y+":
        return (part, {-1: 0, 2: -1}[a], b)
    if way == "y-":
        return (part, {1: 0, 2: 1}[a], b)
    if way == "z+":
        return (part, a, {-1: 0, -2: -1, -3: -2, 4: -3}[b])
    return (part, a, {1: 0, 2: 1, 3: 2, 4: 3}[b])


L_ROWS = {0: {0: (0, 32), 1: (32, 16), 2: (0, 48)}, 1: {0: (48, 32), 1: (80, 48), 2: (48, 80)}}
R_LANES = {0: {0: (0, 128), 1: (128, 128), 2: (0, 256)}, 1: {0: (256, 128), 1: (384, 128), 2: (256, 256)}}


ORDER = [
    ("own",), ("C1",), ("S", 0, 0, -1), ("S", 0, 0, 1), ("L", 1, 0, -1), ("L", 1, 0, 1), ("F",), ("L", 0, -1, 0),
    ("L", 0, 1, 0), ("L", 0, 0, -1), ("L", 0, 0, 1), ("X",), ("S", 0, 0, -2), ("S", 0, 0, 2), ("L", 1, -1, 0),
    ("L", 1, 1, 0), ("S", 0, -1, 0), ("S", 0, 1, 0), ("L", 1, 0, -2), ("L", 1, 0, 2), ("rows",), ("C2",),
    ("L", 1, -1, -1), ("L", 1, 1, -1), ("L", 1, -1, 1), ("L", 1, 1, 1), ("L", 0, 2, 0), ("L", 1, 2, 0),
    ("S", 0, 2, 0), ("L", 0, -1, -1), ("L", 0, -1, 1), ("L", 1, 1, -2), ("L", 1, -1, -2), ("L", 0, 1, -1),
    ("L", 0, 1, 1), ("Rsum",), ("L", 1, 1, 2), ("L", 1, -1, 2), ("L", 0, 0, -2), ("S", 0, 0, -3), ("S", 0, -1, -1),
    ("L", 0, 0, 2), ("S", 0, 1, -1), ("S", 0, 0, 3), ("S", 0, -1, 1), ("S", 0, 1, 1), ("pair", 0, 2), ("L", 1, 2, -1),
    ("L", 1, 2, 1), ("L", 1, 0, -3), ("L", 1, 0, 3), ("L", 1, 2, -2), ("L", 0, 2, -1), ("S", 0, 2, -1),
    ("R", 0, -1, 0), ("L", 0, 2, 1), ("S", 0, 2, 1), ("R", 0, 1, 0), ("R", 1, -1, 0), ("R", 1, 1, 0),
    ("L", 0, -1, -2), ("L", 0, -1, 2), ("CX",), ("L", 1, 2, 2), ("L", 0, 1, -2), ("L", 0, 1, 2), ("R", 0, 0, -1),
    ("R", 0, 0, 1), ("R", 1, 0, -1), ("R", 1, 0, 1), ("L", 0, 0, -3), ("pair", 0, 1), ("S", 0, 0, 4),
    ("L", 1, -1, -3), ("S", 0, -1, -2), ("L", 0, 0, 3), ("L", 1, 1, -3), ("S", 0, 1, -2), ("S", 0, -1, 2),
    ("S", 0, 1, 2), ("L", 1, 0, 4), ("pair", 0, -1), ("R", 0, -1, 1), ("L", 1, -1, 3), ("L", 1, 1, 3),
    ("L", 0, 2, -2), ("S", 0, 2, -2), ("R", 0, 2, 0), ("R", 1, 2, 0), ("R", 0, -1, -1), ("R", 1, -1, -1),
    ("R", 1, 1, -1), ("R", 0, 1, -1), ("L", 0, 2, 2), ("S", 0, 2, 2), ("R", 1, -1, 1), ("R", 1, 1, 1), ("R", 0, 1, 1),
    ("pair", -1, 2), ("L", 0, -1, -3), ("L", 0, -1, 3), ("pair", 1, 2), ("L", 0, 1, -3), ("CW",), ("R", 0, 0, -2),
    ("L", 0, 1, 3), ("L", 1, 2, -3), ("R", 1, 0, -2), ("R", 0, 0, 2), ("R", 1, 0, 2), ("pair", 2, 2),
    ("S", 0, -1, -3), ("L", 0, 0, 4), ("S", 0, 1, -3), ("S", 0, -1, 3), ("S", 0, 1, 3), ("L", 1, -1, 4),
    ("R", 0, -1, 2), ("R", 0, 2, 1), ("L", 1, 1, 4), ("L", 0, 2, -3), ("S", 0, 2, -3), ("pair", -1, 1),
    ("R", 0, 2, -1), ("R", 0, -1, -2), ("L", 0, 2, 3), ("L", 1, 2, 3), ("S", 0, 2, 3), ("R", 1, 2, -1),
    ("R", 0, 1, -2), ("R", 1, 2, 1), ("R", 0, 1, 2), ("pair", 0, 0), ("L", 0, -1, 4), ("R", 1, -1, -2),
    ("R", 1, 1, -2), ("R", 0, 0, 3), ("R", 1, -1, 2), ("R", 1, 1, 2), ("L", 0, 1, 4), ("R", 1, 0, 3), ("R", 0, 0, -3),
    ("pair", 1, 1), ("R", 1, 0, -3), ("S", 0, -1, 4), ("S", 0, 1, 4), ("R", 0, -1, 3), ("R", 0, 2, 2), ("S", 0, 2, 4),
    ("pair", -1, -1), ("L", 1, 2, 4), ("R", 0, 2, -2), ("L", 0, 2, 4), ("R", 0, -1, -3), ("R", 0, 1, 3),
    ("pair", 1, -1), ("R", 0, 1, -3), ("R", 1, 2, -2), ("R", 1, 2, 2), ("pair", 2, 1), ("R", 0, 0, 4),
    ("R", 1, -1, 3), ("R", 1, 1, 3), ("R", 1, 0, 4), ("pair", 2, -1), ("R", 1, -1, -3), ("R", 1, 1, -3),
    ("R", 0, 2, 3), ("pair", -1, 0), ("R", 0, 2, -3), ("R", 0, -1, 4), ("pair", 1, 0), ("R", 0, 1, 4), ("pair", 2, 0),
    ("R", 1, 2, 3), ("R", 1, -1, 4), ("R", 1, 1, 4), ("R", 1, 2, -3), ("R", 0, 2, 4), ("rhs", 0), ("R", 1, 2, 4),
    ("rhs", 1),
]


def dot(a, b, dims):
    return lax.dot_general(a, b, (dims, ((), ())), preferred_element_type=F32)


def split2(v):
    hi = v.astype(BF16)
    return hi, (v - hi.astype(F32)).astype(BF16)


def iota(shape, axis):
    return lax.broadcasted_iota(jnp.int32, shape, axis)


def kernel(gram, inv, cross_h, down_h, removed_h, updated, rhs_out,
           down, removed,
           gt, pt, m_ref, cross, lsrc, ssrc, lall, sall, lrow, srow, rh, rl, ch,
           c0nat, pack, yslot, fbuf, zslot, lost, hh, hl,
           g_sem, in_sem, o_sem, l_send, l_recv, s_send, s_recv, c_send, c_recv, x_send, x_recv,
           p_send, p_recv, y_send, y_recv):
    row, col, tp = lax.axis_index("row"), lax.axis_index("col"), lax.axis_index("tp")
    y, z = row // ZL, tp * ZL + lax.rem(row, ZL)
    xx, core = col // 2, lax.rem(col, 2)

    def slot_of(a, b):
        yy, zz = lax.rem(y + a + NY, NY), lax.rem(z + b + NZ, NZ)
        return yy * 8 + lax.rem(zz, ZL) * 2 + zz // ZL

    def device_of(a, b):
        yy, zz = lax.rem(y + a + NY, NY), lax.rem(z + b + NZ, NZ)
        return {"row": yy * ZL + lax.rem(zz, ZL), "col": col, "tp": zz // ZL}

    def at_col(c):
        return {"row": row, "col": c, "tp": tp}

    def peer_col(off):
        return lax.rem(xx + off, 4) * 2 + core

    to = {"y+": device_of(1, 0), "y-": device_of(-1, 0), "z+": device_of(0, 1), "z-": device_of(0, -1)}
    mine = slot_of(0, 0)

    def remote(src, dst, send, recv, dev):
        return pltpu.make_async_remote_copy(src_ref=src, dst_ref=dst, send_sem=send, recv_sem=recv, device_id=dev, device_id_type=MESH)

    loads = [pltpu.make_async_copy(gram.at[:, j, :], gt.at[j], g_sem.at[j]) for j in range(8)]
    def c0_part(first, count, c):
        return c0nat.at[pl.ds(first, count), c // 2, :, pl.ds(pl.multiple_of(512 * lax.rem(c, 2), 512), 512)]

    c0load = pltpu.make_async_copy(
        cross_h.at[pl.ds(pl.multiple_of(16 * xx, 16), 16), pl.ds(pl.multiple_of(512 * core, 512), 512)],
        c0_part(mine, 1, col).at[0], in_sem.at[0])
    m_load = pltpu.make_async_copy(inv, m_ref, in_sem.at[1])
    x_load = pltpu.make_async_copy(cross_h, cross, in_sem.at[2])

    @pl.when(y < 2)
    def _():
        c0load.start()


    @pl.when(col == 0)
    def _():
        for j in range(8):
            loads[j].start()
    d_load = pltpu.make_async_copy(down_h, down, in_sem.at[3])
    i_load = pltpu.make_async_copy(removed_h, removed, in_sem.at[4])
    i_load.start()
    m_load.start()
    d_load.start()
    x_load.start()

    barrier = pltpu.get_barrier_semaphore()
    others = [device_of(a, 0) for a in (1, 2, 3)] + [device_of(0, b) for b in range(1, 8)]
    others += [at_col(lax.rem(col + off, 8)) for off in range(1, 8)]
    for dev in others:
        pl.semaphore_signal(barrier, inc=1, device_id=dev, device_id_type=MESH)

    class Stream:
        def __init__(self, buf, send, recv, rows, moves):
            self.buf, self.send, self.recv, self.rows, self.moves = buf, send, recv, rows, moves

        def piece(self, t, slot):
            if self.rows is None:
                return self.buf.at[slot]
            start, count = self.rows[t[0]][t[4]]
            return self.buf.at[slot, pl.ds(start, count)]

        def slot(self, a, b):
            return slot_of(a, b)

    class LaneStream(Stream):
        def piece(self, t, slot):
            start, count = self.rows[t[0]][t[4]]
            return self.buf.at[slot, :, pl.ds(start, count)]

        def slot(self, a, b):
            return lax.rem(y + a + NY, NY) * 8 + lax.rem(z + b + NZ, NZ)

    l_st = Stream(lall, l_send, l_recv, L_ROWS, plan(False))
    s_st = Stream(sall, s_send, s_recv, None, plan(True))
    r_st = LaneStream(lost, y_send, y_recv, R_LANES, plan(False))
    started = []

    def copy_of(st, i, slot):
        t = st.moves[i]
        return remote(st.piece(t, slot), st.piece(t, slot), st.send.at[i], st.recv.at[i], to[t[3]])

    def start_from(st, chunk):
        for i, t in enumerate(st.moves):
            if sender_chunk(t) == chunk:
                c = copy_of(st, i, st.slot(chunk[1], chunk[2]))
                c.start()
                started.append(c)

    def wait_for(st, chunk):
        for i, t in enumerate(st.moves):
            if t[:3] == chunk:
                copy_of(st, i, st.slot(chunk[1], chunk[2])).wait_recv()

    def many(copies):
        for c in copies:
            c.start()
        started.extend(copies)
        return copies

    def c0_z():
        return [remote(c0_part(mine, 1, col), c0_part(mine, 1, col), c_send.at[b - 1], c_recv.at[b - 1], device_of(0, b))
                for b in range(1, 8)]

    def c0_y(n):
        block = c0_part(8 * y, 8, col)
        return [remote(block, block, c_send.at[6 + a], c_recv.at[7 + n], device_of(a, 0)) for a in (1, 2, 3)]

    def hand_out(c):
        return [remote(lsrc.at[c], lall.at[mine], x_send.at[c - 1], x_recv.at[0], at_col(c)),
                remote(ssrc.at[c], sall.at[mine], x_send.at[7 + c - 1], x_recv.at[1], at_col(c))]

    eye = iota((64, 128), 0) == iota((64, 128), 1)

    def factor_rows(first):
        r0 = first * 64
        parts = [split2(gt[j, r0:r0 + 128, :]) for j in range(8)]
        hi = jnp.concatenate([p[0] for p in parts], axis=1)
        lo = jnp.concatenate([p[1] for p in parts], axis=1)
        both = jnp.concatenate([hi, lo], axis=0)
        blocks = []
        for n in range(4):
            k = 256 * (n + 1)
            d = dot(both[:, :k], m_ref[256 * n:256 * n + 256, :k], NT)
            blocks.append(d[:128] + d[128:])
        top = jnp.maximum(blocks[0], -blocks[0])
        for b in blocks[1:]:
            top = jnp.maximum(top, jnp.abs(b))
        scale = jnp.maximum(jnp.max(top, axis=1, keepdims=True), 1e-30) / 32767.0
        inverse = 1.0 / scale
        for i in range(2):
            c = first + i
            rows = slice(64 * i, 64 * i + 64)
            for n in range(4):
                q = lax.round(blocks[n][rows] * inverse[rows], lax.RoundingMethod.TO_NEAREST_EVEN)
                q = jnp.clip(q, -32767.0, 32767.0).astype(jnp.int32).astype(I16)
                half, lane = n // 2, 256 * (n % 2)
                lsrc[c, 64 * half:64 * half + 64, lane:lane + 256] = q
            lanes = jnp.sum(jnp.where(eye, jnp.broadcast_to(scale[rows], (64, 128)), 0.0), axis=0, keepdims=True)
            ssrc[c] = jnp.broadcast_to(lanes, (8, 128))

    @pl.when(col == 0)
    def _():
        for j in range(8):
            loads[j].wait()
        m_load.wait()
        factor_rows(6)
        factor_rows(4)

    i_load.wait()
    rem = removed[...]
    flat = jnp.concatenate([rem[i:i + 1, :] for i in range(8)], axis=1)

    def first_of(base):
        less = jnp.where(rem < base, 1.0, 0.0)
        return jnp.sum(jnp.sum(less, axis=1, keepdims=True), axis=0, keepdims=True).astype(jnp.int32)

    shard = down.shape[0]
    base = mine * shard
    place = jnp.where(iota((shard, 1024), 0) == flat - base, 1.0, 0.0).astype(BF16)
    order = jnp.where(iota((128, 1024), 1) - first_of(base) == iota((128, 1024), 0), 1.0, 0.0).astype(BF16)
    pick = dot(order, place, NT).astype(BF16)
    d_load.wait()
    pack[...] = dot(pick, down[...], NN).astype(BF16)
    pl.semaphore_wait(barrier, len(others))

    @pl.when(col == 0)
    def _():
        for c in (6, 4, 7, 5):
            for cp in hand_out(c):
                cp.start()

    @pl.when(y < 2)
    def _():
        c0load.wait()
        for c in c0_z():
            c.start()

    yslot[y] = pack[...]
    ph1 = many([remote(pack, yslot.at[y], p_send.at[a - 1], p_recv.at[a - 1], device_of(a, 0)) for a in (1, 2, 3)])

    @pl.when(col == 0)
    def _():
        for first in (2, 0):
            factor_rows(first)
            for c in range(max(first, 1), first + 2):
                for cp in hand_out(c):
                    cp.start()

    def phase_f():
        for c in ph1:
            c.wait_recv()
        seg = jnp.concatenate([removed[pl.ds(2 * y + i, 1), :] for i in range(2)], axis=1)
        picks = []
        for yy in range(4):
            b = (yy * 8 + lax.rem(mine, 8)) * shard
            inside = (seg >= b) & (seg < b + shard)
            at = jnp.where(inside, iota((1, 256), 1) + 256 * y - first_of(b), -1)
            picks.append(jnp.where(iota((128, 256), 0) == at, 1.0, 0.0).astype(BF16))
        f = dot(jnp.concatenate(picks, axis=0), yslot[...].reshape(512, 512), TN).astype(BF16)
        for i in range(8):
            fbuf[i] = f[32 * i:32 * i + 32]
        zslot[z] = fbuf[z]
        return many([remote(fbuf.at[lax.rem(z + b, 8)], zslot.at[z], p_send.at[3 + b - 1], p_recv.at[3 + b - 1], device_of(0, b))
                     for b in range(1, 8)])

    def phase_r(ph2):
        for c in ph2:
            c.wait_recv()
        total = zslot[0].astype(F32)
        for i in range(1, 8):
            total = total + zslot[i].astype(F32)
        lost[y * 8 + z] = total.astype(BF16)
        for part in (0, 1):
            start_from(r_st, (part, 0, 0))

    def x_peers(n, src, dst):
        return many([remote(src, dst.at[col], x_send.at[14 + 7 * n + off - 1], x_recv.at[2 + 7 * n + off - 1], at_col(peer_col(off)))
                     for off in range(1, 4)])

    def to_sibling(n, off, src, dst, slot):
        return many([remote(src, dst.at[slot], x_send.at[14 + 7 * n + 3 + off], x_recv.at[2 + 7 * n + 3 + off], at_col(col + 1 - 2 * core))])

    state = {}

    def own_rows():
        @pl.when(col == 0)
        def _():
            lall[mine] = lsrc[0]
            sall[mine] = ssrc[0]

        @pl.when(col != 0)
        def _():
            for k, dst in enumerate((lall, sall)):
                remote(dst.at[mine], dst.at[mine], x_send.at[0], x_recv.at[k], to["y+"]).wait_recv()
        for part in (0, 1):
            start_from(l_st, (part, 0, 0))
        start_from(s_st, (0, 0, 0))
        lrow[col] = lall[mine]
        srow[col] = sall[mine]
        state["xl"] = x_peers(0, lrow.at[col], lrow)
        state["xs"] = x_peers(1, srow.at[col], srow)
        state["sl"] = to_sibling(0, 0, lrow.at[col], lrow, col)
        state["ss"] = to_sibling(1, 0, srow.at[col], srow, col)

    def forward_rows(n, key, skey, buf):
        for off in range(1, 4):
            state[key][off - 1].wait_recv()
            c = lax.rem(xx - off + 4, 4) * 2 + core
            state[skey] += to_sibling(n, off, buf.at[c], buf, c)

    def dequant(q_ref, s_ref, slot):
        s = jnp.sum(jnp.where(eye, jnp.broadcast_to(s_ref[slot, 0:1, :], (64, 128)), 0.0), axis=1, keepdims=True)
        v = jnp.concatenate([q_ref[slot, 0:64, :], q_ref[slot, 64:128, :]], axis=1)
        return split2(v.astype(jnp.int32).astype(F32) * s)

    def rows_ready():
        for k in ("sl", "ss"):
            for c in state[k]:
                c.wait_recv()

        def body(c, _):
            hi, lo = dequant(lrow, srow, c)
            at = pl.ds(pl.multiple_of(64 * c, 64), 64)
            rh[at, :] = hi
            rl[at, :] = lo
            return 0
        lax.fori_loop(0, 8, body, 0)

    outs = []

    def columns(n, a, b):
        yy, zl = lax.rem(y + a + NY, NY), lax.rem(z + b + NZ, ZL)
        j = yy * 4 + zl
        for i in range(2):
            hi, lo = dequant(lall, sall, 2 * j + i)
            ch[64 * i:64 * i + 64, :] = hi
            ch[128 + 64 * i:192 + 64 * i, :] = lo
        p = dot(rh[...], ch[...], NT)
        p = p[:, :128] + p[:, 128:] + dot(rl[...], ch[:128], NT)
        pt[j] = p
        cp = pltpu.make_async_copy(pt.at[j], updated.at[:, j, :], o_sem.at[n])
        cp.start()
        outs.append(cp)

    def right_side(part):
        lanes = slice(256 * part, 256 * part + 256)
        r_hi, r_lo = split2(dot(c0nat[...].reshape(1024, 1024), lost[:, :, lanes].reshape(1024, 256), NN))
        for n in range(4):
            k = 256 * (n + 1)
            mm = m_ref[256 * n:256 * n + 256, :k]
            hi, lo = split2(dot(mm, r_hi[:k], NN) + dot(mm, r_lo[:k], NN))
            hh[256 * n:256 * n + 256, :] = hi
            hl[256 * n:256 * n + 256, :] = lo
        rhs = dot(cross[...], lost[:, :, lanes].reshape(1024, 256), NN)
        rhs_out[:, lanes] = rhs - (dot(rh[...], hh[...], NN) + dot(rh[...], hl[...], NN) + dot(rl[...], hh[...], NN))

    def c0_across():
        @pl.when(y < 2)
        def _():
            for c in c0_z():
                c.wait_recv()

        for n in range(2):
            @pl.when(y == n)
            def _():
                for c in c0_y(n):
                    c.start()

    def c0_done():
        for n in range(2):
            @pl.when(y != n)
            def _():
                block = c0_part(8 * n, 8, col)
                remote(block, block, c_send.at[0], c_recv.at[7 + n], to["y+"]).wait_recv()
        own = c0_part(0, 16, col)
        state["xc"] = many([remote(own, own, x_send.at[28 + off - 1], x_recv.at[16 + off - 1], at_col(peer_col(off))) for off in range(1, 4)])
        state["sc"] = many([remote(own, own, x_send.at[31], x_recv.at[19], at_col(col + 1 - 2 * core))])

    def c0_forward():
        for off in range(1, 4):
            state["xc"][off - 1].wait_recv()
            block = c0_part(0, 16, lax.rem(xx - off + 4, 4) * 2 + core)
            state["sc"] += many([remote(block, block, x_send.at[31 + off], x_recv.at[19 + off], at_col(col + 1 - 2 * core))])

    def loaded():
        @pl.when(col != 0)
        def _():
            m_load.wait()

    streams = {"L": l_st, "R": r_st, "S": s_st}
    steps = {
        "own": own_rows,
        "F": lambda: state.update(ph2=phase_f()),
        "Rsum": lambda: phase_r(state["ph2"]),
        "C1": c0_across,
        "C2": c0_done,
        "CX": c0_forward,
        "CW": lambda: ([c.wait_recv() for c in state["sc"]], x_load.wait()),
        "X": lambda: (forward_rows(1, "xs", "ss", srow), forward_rows(0, "xl", "sl", lrow)),
        "rows": lambda: (loaded(), rows_ready()),
            }
    pairs = 0
    for event in ORDER:
        if event[0] in streams:
            wait_for(streams[event[0]], event[1:])
            start_from(streams[event[0]], event[1:])
        elif event[0] == "rhs":
            right_side(event[1])
        elif event[0] == "pair":
            columns(pairs, event[1], event[2])
            pairs += 1
        else:
            steps[event[0]]()
    for c in started:
        c.wait_send()
    for c in outs:
        c.wait()

    @pl.when(y < 2)
    def _():
        for c in c0_z() + c0_y(0):
            c.wait_send()

    @pl.when(col == 0)
    def _():
        for c in range(1, 8):
            for cp in hand_out(c):
                cp.wait_send()


def per_device(gram, inv_factor, cross_gram, down_rows, removed):
    vm = pl.BlockSpec(memory_space=pltpu.VMEM)
    hbm = pl.BlockSpec(memory_space=pl.ANY)
    dma = pltpu.SemaphoreType.DMA
    big, small = len(plan(False)), len(plan(True))
    v = pltpu.VMEM
    updated, rhs = pl.pallas_call(
        kernel,
        out_shape=[jax.ShapeDtypeStruct((512, 16, 128), F32), jax.ShapeDtypeStruct((512, 512), F32)],
        in_specs=[hbm] * 5,
        out_specs=[hbm, vm],
        scratch_shapes=[
            v(down_rows.shape, BF16), v((8, 128), jnp.int32), v((8, 512, 128), F32), v((16, 512, 128), F32), v((1024, 1024), BF16), v((512, 1024), BF16),
            v((8, 128, 512), I16), v((8, 8, 128), F32), v((32, 128, 512), I16), v((32, 8, 128), F32),
            v((8, 128, 512), I16), v((8, 8, 128), F32), v((512, 1024), BF16), v((512, 1024), BF16),
            v((256, 1024), BF16),
            v((16, 4, 16, 1024), BF16), v((128, 512), BF16), v((4, 128, 512), BF16),
            v((8, 32, 512), BF16), v((8, 32, 512), BF16), v((32, 32, 512), BF16),
            v((1024, 256), BF16), v((1024, 256), BF16),
            dma((8,)), dma((5,)), dma((16,)), dma((big,)), dma((big,)), dma((small,)), dma((small,)),
            dma((10,)), dma((9,)), dma((35,)), dma((23,)), dma((10,)), dma((10,)), dma((big,)), dma((big,)),
        ],
        cost_estimate=pl.CostEstimate(flops=15_000_000_000, bytes_accessed=13_000_000, transcendentals=0),
        compiler_params=pltpu.CompilerParams(collective_id=0, has_side_effects=True, vmem_limit_bytes=56 << 20),
    )(gram.reshape(512, 16, 128), inv_factor, cross_gram.reshape(512, 1024), down_rows, removed.reshape(8, 128))
    updated = gram.reshape(512, 16, 128) - updated
    return (updated.reshape(gram.shape), rhs.reshape(8, 1, 64, 512))


def solution(mesh):
    return jax.shard_map(
        per_device,
        mesh=mesh,
        in_specs=(
            P(None, "row", "tp", None, "col", None),
            P(),
            P(None, "row", "tp", None),
            P(("row", "tp"), "col"),
            P(),
        ),
        out_specs=(P(None, "row", "tp", None, "col", None), P(None, "row", "tp", "col")),
        check_vma=False,
    )
```
